128 devices in a mesh: lat: 32 (over z, y, core), dp: 4 (over x).
Axes of the slice: x: 4, y: 4, z: 4, core: 2. Of those that a mesh axis runs over, the one named last changes fastest.
Arguments:
- buffer: bfloat16 [4096, 3584], P(('lat', 'dp')), may hold values from -6 to 6
- row_ids: int32 [2, 1024], P(None, ('lat', 'dp')), may hold values from 0 to 31
- enc_weight: bfloat16 [3584, 8192], P(None, 'lat'), may hold values from -0.09375 to 0.09375
- dec_weight: bfloat16 [8192, 3584], P('lat'), may hold values from -0.0625 to 0.0625
- threshold_codes: int32 [8192], P('lat'), may hold values from 0 to 15
- dead_mask: int32 [8192], P('lat'), may hold values 0 or 1
- enc_second: float32 [3584, 8192], P('dp', 'lat'), may hold values from 9.765625e-08 to 9.765625e-06
- dec_second: float32 [8192, 3584], P('lat', 'dp'), may hold values from 9.765625e-08 to 9.765625e-06
Outputs:
- enc_update: float32 [3584, 8192], P('dp', 'lat')
- enc_second_new: float32 [3584, 8192], P('dp', 'lat')
- dec_update: float32 [8192, 3584], P('lat', 'dp')
- dec_second_new: float32 [8192, 3584], P('lat', 'dp')
- losses: float32 [2, 2], replicated
The draws below stay inside these ranges and needn't reach their ends.
Inputs may be any that keep to these rules, and one draw needn't show every extreme that they name: row_ids[m, r] names a row inside the block of 32 buffer rows numbered r // 8.
All inputs are finite; a program needn't handle non-finite values. No bound on the sum of `dead_mask` on one device may be relied on, other than what follows from the above.
Results may differ from the reference program's by a relative error of at most 0.012.
Values may be sent and summed in bfloat16 or wider, within the bound.
No kernel may reach another device: no remote copies, remote signals or barrier semaphores. Data moves between devices by JAX's collectives and lax.ppermute only.
A program may use at most 64 MiB of HBM per device.

```python
import math
import jax
import jax.numpy as jnp
from jax import lax

D = 3584
MB_TOK = 256
MICRO = 2
LATENTS = 8192
TOKENS_MB = 1024
BUF_DEV = 32
N_LAT = 32
N_DP = 4


def plant(values, rng, least, top_value):
    longest = values.shape.index(max(values.shape))
    spots = []
    for shift in (0, 1):
        where = [jax.random.randint(jax.random.fold_in(rng, axis), (), 0, length) for axis, length in enumerate(values.shape)]
        where[longest] = (where[longest] + shift) % values.shape[longest]
        spots.append(tuple(where))
    return values.at[spots[0]].set(least).at[spots[1]].set(top_value)


def block_scale(key, extent, shards, smallest, high):
    factor_of = 1.0
    for axis_at, parts in shards:
        steps = jax.random.uniform(jax.random.fold_in(jax.random.fold_in(key, 6), axis_at), (parts,), jnp.float32, smallest / len(shards), high / len(shards))
        factor_of = factor_of * jnp.repeat(jnp.exp(steps), extent[axis_at] // parts).reshape((-1,) + (1,) * (len(extent) - 1 - axis_at))
    return factor_of


def gaussian(rng, extent, spread, limit, pieces=(), kind=jnp.bfloat16):
    values = jax.random.normal(rng, extent, jnp.float32) * spread
    if len(pieces) > 0:
        values = block_scale(rng, extent, pieces, -0.22, 0.18) * values
    return jnp.clip(values, min=-limit, max=limit).astype(kind)


def setup_inputs(seed: int = 0) -> dict:
    seeds = jax.random.split(jax.random.key(seed), 9)
    buffer = gaussian(seeds[0], (BUF_DEV * N_LAT * N_DP, D), 1.0, 6.0, ((0, 128),))
    row_ids = plant(jax.random.randint(seeds[1], (MICRO, TOKENS_MB), 0, BUF_DEV), jax.random.fold_in(seeds[1], 1), 0, BUF_DEV - 1).astype(jnp.int32)
    enc_weight = gaussian(seeds[2], (D, LATENTS), D ** -0.5, 0.09375, ((1, 32),))
    dec_weight = gaussian(seeds[3], (LATENTS, D), LATENTS ** -0.5, 0.0625, ((0, 32),))
    threshold_codes = plant(jax.random.randint(seeds[4], (LATENTS,), 0, 16), jax.random.fold_in(seeds[4], 1), 0, 15).astype(jnp.int32)
    dead_mask = plant((jax.random.randint(seeds[5], (LATENTS,), 0, 4) < 1).astype(jnp.int32), jax.random.fold_in(seeds[5], 1), 0, 1)
    enc_second = jnp.clip(jnp.exp(math.log(9.765624781721272e-06) - 4.6051702 * jax.random.uniform(seeds[6], (D, LATENTS), jnp.float32) ** block_scale(seeds[6], (D, LATENTS), ((0, 4), (1, 32)), -0.2, 0.2)), 9.765624753299562e-08, 9.765624781721272e-06)
    dec_second = jnp.clip(jnp.exp(math.log(9.765624781721272e-06) - 4.6051702 * jax.random.uniform(seeds[7], (LATENTS, D), jnp.float32) ** block_scale(seeds[7], (LATENTS, D), ((0, 32), (1, 4)), -0.2, 0.2)), 9.765624753299562e-08, 9.765624781721272e-06)
    return {"buffer": buffer, "row_ids": row_ids, "enc_weight": enc_weight, "dec_weight": dec_weight, "threshold_codes": threshold_codes, "dead_mask": dead_mask, "enc_second": enc_second, "dec_second": dec_second}


gate_width = 0.1
code_step = 0.1
norm_eps = 1e-06
beta_two = 0.999
adam_eps = 1e-08
adam_count = 2000

def adam_second(grads, second):
    renewed = beta_two * second + (1.0 - beta_two) * grads * grads
    correction = 1.0 - beta_two ** adam_count
    return (grads / (jnp.sqrt(renewed / correction) + adam_eps), renewed)

def contract(left, right, dim):
    return lax.dot_general(left, right, (((dim,), (dim,)), ((), ())), preferred_element_type=jnp.float32)

def reference(buffer, row_ids, enc_weight, dec_weight, threshold_codes, dead_mask, enc_second, dec_second):
    micro_count, token_count = row_ids.shape
    own_rows = MB_TOK // N_LAT
    block_base = jnp.arange(token_count, dtype=jnp.int32) // own_rows * BUF_DEV
    token_total = micro_count * token_count
    thresh = code_step * threshold_codes.astype(jnp.float32)
    dead_flags = dead_mask.astype(jnp.float32)
    enc_grad = jnp.zeros(enc_weight.shape, jnp.float32)
    dec_grad = jnp.zeros(dec_weight.shape, jnp.float32)
    recon_list = []
    ghost_list = []
    for micro_index in range(micro_count):
        tokens = buffer[(block_base + row_ids[micro_index]).astype(jnp.int32)]
        preact = jnp.dot(tokens, enc_weight, preferred_element_type=jnp.float32)
        gating = jax.nn.sigmoid((preact - thresh) / gate_width)
        active = (preact * gating).astype(jnp.bfloat16)
        raised = jnp.exp(preact) * dead_flags
        ghost_act = raised.astype(jnp.bfloat16)
        rebuilt = jnp.dot(active, dec_weight, preferred_element_type=jnp.float32)
        ghost_out = jnp.dot(ghost_act, dec_weight, preferred_element_type=jnp.float32)
        residual = tokens.astype(jnp.float32) - rebuilt
        ghost_scale = jnp.sqrt(lax.optimization_barrier(jnp.sum(residual * residual, axis=1)) + norm_eps) / (2.0 * jnp.sqrt(lax.optimization_barrier(jnp.sum(ghost_out * ghost_out, axis=1)) + norm_eps))
        ghost_diff = ghost_scale[:, None] * ghost_out - residual
        recon_loss = jnp.sum(residual * residual) / token_total
        ghost_loss = jnp.sum(ghost_diff * ghost_diff) / token_total
        ratio = recon_loss / ghost_loss
        recon_list.append(recon_loss)
        ghost_list.append(ghost_loss)
        recon_grad = (residual * (-2.0 / token_total)).astype(jnp.bfloat16)
        ghost_grad = (ghost_diff * ghost_scale[:, None] * (2.0 / token_total)).astype(jnp.bfloat16)
        latent_grad = contract(recon_grad, dec_weight, 1)
        ghost_latent = ratio * contract(ghost_grad, dec_weight, 1)
        pre_grad = (latent_grad * (gating + preact * gating * (1.0 - gating) / gate_width) + ghost_latent * raised).astype(jnp.bfloat16)
        enc_grad = enc_grad + contract(tokens, pre_grad, 0)
        dec_grad = dec_grad + contract(active, recon_grad, 0) + ratio * contract(ghost_act, ghost_grad, 0)
    enc_update, enc_second_new = adam_second(enc_grad, enc_second)
    dec_update, dec_second_new = adam_second(dec_grad, dec_second)
    losses = jnp.stack([jnp.stack(recon_list), jnp.stack(ghost_list)])
    return (enc_update, enc_second_new, dec_update, dec_second_new, losses)
```

```python
import jax
import jax.numpy as jnp
from jax import lax
from jax.sharding import Mesh
from jax.sharding import PartitionSpec as P

AXES = ("z", "y", "c", "x")
LAT = ("z", "y", "c")
LAT_DP = ("z", "y", "c", "x")


gate_width = 0.1
code_step = 0.1
norm_eps = 1e-06
beta_two = 0.999
adam_eps = 1e-08
adam_count = 2000

ORDER = (
    ((("y", 1), ("z", 1), ("y", 3), ("z", 3)), (("y", 3), ("z", 3), ("y", 1), ("z", 1))),
    ((("z", 1), ("y", 1), ("z", 3), ("y", 3)), (("z", 3), ("y", 3), ("z", 1), ("y", 1))),
)
STAGES = 4


def adam_second(grads, second):
    renewed = beta_two * second + (1.0 - beta_two) * grads * grads
    correction = 1.0 - beta_two**adam_count
    return (grads / (jnp.sqrt(renewed / correction) + adam_eps), renewed)


def contract(left, right, dim):
    return lax.dot_general(
        left, right, (((dim,), (dim,)), ((), ())), preferred_element_type=jnp.float32
    )


def neighbours(stage, micro):
    pairs = []
    for z in range(4):
        for y in range(4):
            for c in range(2):
                axis, mask = ORDER[c][micro][stage]
                to_z, to_y = (z ^ mask, y) if axis == "z" else (z, y ^ mask)
                pairs.append((z * 8 + y * 2 + c, to_z * 8 + to_y * 2 + c))
    return pairs


def swap_stage(value, stage, micro):
    return lax.ppermute(value, LAT, neighbours(stage, micro))


def swap_cores(value):
    return lax.ppermute(value, "c", [(0, 1), (1, 0)])


def swap_groups(value, mask):
    return lax.ppermute(value, "x", [(i, i ^ mask) for i in range(4)])


def gather_stages(value, micro):
    for stage in range(STAGES):
        value = jnp.concatenate([value, swap_stage(value, stage, micro)], axis=0)
    return value


def add_rounded(mine, theirs):
    return (mine.astype(jnp.float32) + theirs.astype(jnp.float32)).astype(jnp.bfloat16)


def reduce_stages(mine, theirs, micro):
    for stage in reversed(range(STAGES)):
        half = mine.shape[0] // 2
        sent = add_rounded(mine[half:], theirs[half:])
        mine = add_rounded(mine[:half], theirs[:half])
        theirs = swap_stage(sent, stage, micro)
    return mine.astype(jnp.float32) + theirs.astype(jnp.float32)


def own_quarter_first(value, dim, group):
    width = value.shape[dim] // 4
    return jnp.concatenate(
        [lax.dynamic_slice_in_dim(value, (group ^ m) * width, width, dim) for m in (0, 1, 3, 2)],
        axis=dim,
    )


def reduce_groups(grads):
    width = grads.shape[1] // 4
    rows = grads.shape[0] // 2
    quarter = [grads[:, k * width : (k + 1) * width] for k in range(4)]

    def pick(slots, first):
        return [quarter[k][:rows] if first else quarter[k][rows:] for k in slots]

    def exchange(kept, sent, outer, inner, first):
        kept, sent = pick(kept, first), pick(sent, first)
        got = swap_groups(jnp.concatenate([s.astype(jnp.bfloat16) for s in sent], 0), outer)
        got = got.astype(jnp.float32)
        last = swap_groups((kept[1] + got[rows:]).astype(jnp.bfloat16), inner)
        return kept[0] + got[:rows] + last.astype(jnp.float32)

    return jnp.concatenate(
        [exchange((0, 1), (2, 3), 3, 1, True), exchange((0, 2), (1, 3), 1, 3, False)], axis=0
    )


def interleave(first, second, rows):
    width = first.shape[1]
    both = jnp.stack([first.reshape(-1, rows, width), second.reshape(-1, rows, width)], axis=1)
    return both.reshape(-1, width)


def shards(
    buffer, row_ids, enc_weight, dec_weight, threshold_codes, dead_mask, enc_second, dec_second
):
    micros, rows = row_ids.shape
    token_total = micros * rows * 128
    group = lax.axis_index("x")
    thresh = code_step * threshold_codes.astype(jnp.float32)
    dead_flags = dead_mask.astype(jnp.float32)
    enc = own_quarter_first(enc_weight, 0, group)
    dec = own_quarter_first(dec_weight, 1, group)
    own = [own_quarter_first(buffer[row_ids[m]], 1, group) for m in range(micros)]
    tokens = []
    for m in range(micros):
        mine = gather_stages(own[m], m)
        tokens.append((mine, swap_cores(mine)))

    def forward(block):
        preact = jnp.dot(block, enc, preferred_element_type=jnp.float32)
        gating = jax.nn.sigmoid((preact - thresh) / gate_width)
        active = (preact * gating).astype(jnp.bfloat16)
        raised = jnp.exp(preact) * dead_flags
        ghost_act = raised.astype(jnp.bfloat16)
        partial = jnp.dot(
            interleave(active, ghost_act, rows), dec, preferred_element_type=jnp.float32
        ).astype(jnp.bfloat16)
        return (preact, gating, active, raised, ghost_act), partial

    saved = []
    outs = []
    for m in range(micros):
        theirs_saved, theirs_partial = forward(tokens[m][1])
        got = swap_cores(theirs_partial)
        mine_saved, mine_partial = forward(tokens[m][0])
        saved.append((mine_saved, theirs_saved))
        summed = reduce_stages(mine_partial, got, m)
        residual = own[m].astype(jnp.float32) - summed[:rows]
        both = jnp.concatenate([residual, summed[rows:]], axis=0).astype(jnp.bfloat16)
        mine = gather_stages(both, m)
        outs.append((mine, swap_cores(mine)))

    def token_sums(both):
        split = both.reshape(-1, 2, rows, both.shape[1]).astype(jnp.float32)
        residual, ghost = split[:, 0], split[:, 1]
        rr = jnp.sum(residual * residual, axis=2).reshape(-1, 1)
        gg = jnp.sum(ghost * ghost, axis=2).reshape(-1, 1)
        rg = jnp.sum(residual * ghost, axis=2).reshape(-1, 1)
        scale = jnp.sqrt(rr + norm_eps) / (2.0 * jnp.sqrt(gg + norm_eps))
        cross = jnp.where(scale > 0.0, scale * (scale * gg - 2.0 * rg), 0.0)
        return scale, jnp.sum(rr), jnp.sum(rr + cross)

    scales = []
    parts = []
    for m in range(micros):
        mine, theirs = token_sums(outs[m][0]), token_sums(outs[m][1])
        scales.append((mine[0], theirs[0]))
        parts += [mine[1] + theirs[1], mine[2] + theirs[2]]
    sums = jnp.stack(parts).reshape(1, -1)
    sums = sums + swap_groups(sums, 1)
    sums = sums + swap_groups(sums, 3)

    dec_grad = None
    enc_grad = None
    factor = -2.0 / token_total
    dec_pieces = []
    enc_pieces = []
    for m in range(micros):
        ratio = sums[0, 2 * m] / sums[0, 2 * m + 1]
        for side in range(2):
            preact, gating, active, raised, ghost_act = saved[m][side]
            both = outs[m][side]
            scale = scales[m][side]
            back = contract(both, dec, 1).reshape(-1, 2, rows, dec.shape[0])
            from_residual = back[:, 0].reshape(-1, dec.shape[0])
            from_ghost = back[:, 1].reshape(-1, dec.shape[0])
            ghost_back = scale * (jnp.where(scale > 0.0, scale * from_ghost, 0.0) - from_residual)
            pre_grad = (
                from_residual * (gating + preact * gating * (1.0 - gating) / gate_width)
                - ratio * ghost_back * raised
            ).astype(jnp.bfloat16)
            weighted = ratio * (scale * ghost_act.astype(jnp.float32))
            sides = interleave(
                (active.astype(jnp.float32) + weighted).astype(jnp.bfloat16),
                (-(scale * weighted)).astype(jnp.bfloat16),
                rows,
            )
            dec_pieces.append((sides, both))
            enc_pieces.append((pre_grad, tokens[m][side]))

    def total(pieces):
        out = contract(pieces[0][0], pieces[0][1], 0)
        for left, right in pieces[1:]:
            out = out + contract(left, right, 0)
        return out

    dec_grad = reduce_groups(total(dec_pieces)) * factor
    enc_grad = (reduce_groups(total(enc_pieces)) * factor).T
    dec_update, dec_second_new = adam_second(dec_grad, dec_second)
    enc_update, enc_second_new = adam_second(enc_grad, enc_second)
    losses = (sums.reshape(micros, 2) / token_total).T
    return (enc_update, enc_second_new, dec_update, dec_second_new, losses)


def solution(mesh):
    finer = Mesh(mesh.devices.reshape(4, 4, 2, 4), AXES)
    in_specs = (
        P(LAT_DP, None),
        P(None, LAT_DP),
        P(None, LAT),
        P(LAT, None),
        P(LAT),
        P(LAT),
        P("x", LAT),
        P(LAT, "x"),
    )
    out_specs = (P("x", LAT), P("x", LAT), P(LAT, "x"), P(LAT, "x"), P())
    return jax.shard_map(
        shards, mesh=finer, in_specs=in_specs, out_specs=out_specs, check_vma=False
    )
```

```python
import jax
import jax.numpy as jnp
from jax import lax
from jax.experimental import pallas as pl
from jax.experimental.pallas import tpu as pltpu
from jax.sharding import Mesh
from jax.sharding import PartitionSpec as P

AXES = ("z", "y", "c", "x")
LAT = ("z", "y", "c")
LAT_DP = ("z", "y", "c", "x")


gate_width = 0.1
code_step = 0.1
norm_eps = 1e-06
beta_two = 0.999
adam_eps = 1e-08
adam_count = 2000

ORDER = (
    ((("y", 1), ("z", 1), ("y", 3), ("z", 3)), (("y", 1), ("z", 1), ("z", 3), ("y", 3))),
    ((("y", 3), ("z", 3), ("y", 1), ("z", 1)), (("y", 3), ("z", 3), ("z", 1), ("y", 1))),
)
JOINT = 2
STAGES = 4
EXTRA = 128


def adam_second(grads, second):
    renewed = beta_two * second + (1.0 - beta_two) * grads * grads
    correction = 1.0 - beta_two**adam_count
    return (grads / (jnp.sqrt(renewed / correction) + adam_eps), renewed)


def neighbours(stage, micro):
    pairs = []
    for z in range(4):
        for y in range(4):
            for c in range(2):
                axis, mask = ORDER[c][micro][stage]
                to_z, to_y = (z ^ mask, y) if axis == "z" else (z, y ^ mask)
                pairs.append((z * 8 + y * 2 + c, to_z * 8 + to_y * 2 + c))
    return pairs


def swap_stage(value, stage, micro):
    return lax.ppermute(value, LAT, neighbours(stage, micro))


def swap_cores(value):
    return lax.ppermute(value, "c", [(0, 1), (1, 0)])


def swap_groups(value, mask):
    return lax.ppermute(value, "x", [(i, i ^ mask) for i in range(4)])


def gather_stages(value):
    for stage in range(JOINT):
        value = jnp.concatenate([value, swap_stage(value, stage, 0)], axis=1)
    blocks = [value[0], value[1]]
    for stage in range(JOINT, STAGES):
        theirs = lax.optimization_barrier([swap_stage(b, stage, m) for m, b in enumerate(blocks)])
        blocks = [jnp.concatenate([b, t], axis=0) for b, t in zip(blocks, theirs)]
    return blocks


def add_rounded(mine, theirs):
    return (mine.astype(jnp.float32) + theirs.astype(jnp.float32)).astype(jnp.bfloat16)


def reduce_stages(mine, theirs):
    for stage in reversed(range(STAGES)):
        half = mine[0].shape[0] // 2
        sent = [add_rounded(a[half:], b[half:]) for a, b in zip(mine, theirs)]
        mine = [add_rounded(a[:half], b[:half]) for a, b in zip(mine, theirs)]
        if stage < JOINT:
            theirs = swap_stage(jnp.stack(sent), stage, 0)
            theirs = [theirs[0], theirs[1]]
        else:
            theirs = lax.optimization_barrier([swap_stage(v, stage, m) for m, v in enumerate(sent)])
    return [a.astype(jnp.float32) + b.astype(jnp.float32) for a, b in zip(mine, theirs)]


def in_parts(value):
    high = lax.reduce_precision(value, 8, 7)
    middle = lax.reduce_precision(value - high, 8, 7)
    return [high, middle, value - high - middle]


def vmem(count):
    return [pl.BlockSpec(memory_space=pltpu.VMEM)] * count


def back_kernel(both_ref, dec_ref, back_ref):
    width = dec_ref.shape[1]
    back_ref[...] = lax.dot_general(
        both_ref[:, :width],
        dec_ref[...],
        (((1,), (1,)), ((), ())),
        preferred_element_type=jnp.float32,
    )


def back_project(both, dec):
    shape = (both.shape[0], dec.shape[0])
    return pl.pallas_call(
        back_kernel,
        out_shape=jax.ShapeDtypeStruct(shape, jnp.float32),
        in_specs=vmem(2),
        out_specs=pl.BlockSpec(memory_space=pltpu.VMEM),
        cost_estimate=pl.CostEstimate(
            flops=2 * shape[0] * shape[1] * dec.shape[1],
            bytes_accessed=2 * (both.size + dec.size) + 4 * shape[0] * shape[1],
            transcendentals=0,
        ),
        name="back",
    )(both, dec)


def write_grads(lefts, rights, width, send_a, send_b, keep_a, keep_b):
    rows = keep_a.shape[1]
    for slot in range(4):
        grads = None
        for left, right in zip(lefts, rights):
            term = jnp.dot(
                left,
                right[:, slot * width : (slot + 1) * width],
                preferred_element_type=jnp.float32,
            )
            grads = term if grads is None else grads + term
        top, bottom = grads[:rows], grads[rows:]
        if slot < 2:
            keep_a[slot] = top
        else:
            send_a[(slot - 2) * rows : (slot - 1) * rows, :] = top.astype(jnp.bfloat16)
        if slot % 2 == 0:
            keep_b[slot // 2] = bottom
        else:
            at = slot // 2
            send_b[at * rows : (at + 1) * rows, :] = bottom.astype(jnp.bfloat16)


def grad_shapes(latents, width):
    return [jax.ShapeDtypeStruct((latents, width), jnp.bfloat16)] * 2 + [
        jax.ShapeDtypeStruct((2, latents // 2, width), jnp.float32)
    ] * 2


def dec_kernel(rows, sums_ref, thresh_ref, dead_ref, *refs):
    preacts, backs, boths = refs[0:4], refs[4:8], refs[8:12]
    pre_grads, outs = refs[12:16], refs[16:]
    latents = thresh_ref.shape[1]
    features = boths[0].shape[1] - EXTRA
    lefts = []
    for i in range(4):
        micro = i // 2
        ratio = sums_ref[0, micro] / sums_ref[1, micro]
        preact = preacts[i][...]
        gating = jax.nn.sigmoid((preact - thresh_ref[...]) / gate_width)
        raised = jnp.exp(preact) * dead_ref[...]
        active = (preact * gating).astype(jnp.bfloat16).astype(jnp.float32)
        ghost_act = raised.astype(jnp.bfloat16).astype(jnp.float32)
        extra = boths[i][:, features:].astype(jnp.float32).reshape(-1, 2, rows, EXTRA)
        extra = extra[:, 0].reshape(-1, EXTRA)
        scale = extra[:, 0:1] + extra[:, 1:2] + extra[:, 2:3]
        back = backs[i][...].reshape(-1, 2, rows, latents)
        from_residual = back[:, 0].reshape(-1, latents)
        from_ghost = back[:, 1].reshape(-1, latents)
        ghost_back = scale * (jnp.where(scale > 0.0, scale * from_ghost, 0.0) - from_residual)
        pre_grad = (
            from_residual * (gating + preact * gating * (1.0 - gating) / gate_width)
            - ratio * ghost_back * raised
        )
        pre_grads[i][...] = pre_grad.T.astype(jnp.bfloat16)
        weighted = ratio * (scale * ghost_act)
        pair = (active + weighted).reshape(-1, 1, rows, latents)
        pair = jnp.concatenate([pair, -(scale * weighted).reshape(-1, 1, rows, latents)], axis=1)
        lefts.append(pair.reshape(-1, latents).T.astype(jnp.bfloat16))
    write_grads(lefts, boths, features // 4, *outs)


def dec_grads(rows, sums, thresh, dead_flags, preacts, backs, boths):
    latents = thresh.shape[1]
    width = (boths[0].shape[1] - EXTRA) // 4
    out_shape = [
        jax.ShapeDtypeStruct((latents, p.shape[0]), jnp.bfloat16) for p in preacts
    ] + grad_shapes(latents, width)
    outs = pl.pallas_call(
        lambda *refs: dec_kernel(rows, *refs),
        out_shape=out_shape,
        in_specs=[pl.BlockSpec(memory_space=pltpu.SMEM)] + vmem(14),
        out_specs=vmem(8),
        cost_estimate=pl.CostEstimate(
            flops=8 * latents * width * 4 * boths[0].shape[0],
            bytes_accessed=8 * boths[0].size + 24 * latents * width,
            transcendentals=0,
        ),
        name="decoder_gradient",
    )(sums, thresh, dead_flags, *preacts, *backs, *boths)
    return outs[:4], outs[4:]


def enc_kernel(*refs):
    write_grads([r[...] for r in refs[0:4]], refs[4:8], refs[4].shape[1] // 4, *refs[8:])


def enc_grads(pre_grads, tokens):
    latents = pre_grads[0].shape[0]
    width = tokens[0].shape[1] // 4
    return pl.pallas_call(
        enc_kernel,
        out_shape=grad_shapes(latents, width),
        in_specs=vmem(8),
        out_specs=vmem(4),
        cost_estimate=pl.CostEstimate(
            flops=8 * latents * width * 4 * tokens[0].shape[0],
            bytes_accessed=8 * tokens[0].size + 24 * latents * width,
            transcendentals=0,
        ),
        name="encoder_gradient",
    )(*pre_grads, *tokens)


def own_quarter_first(value, dim, group):
    width = value.shape[dim] // 4
    return jnp.concatenate(
        [lax.dynamic_slice_in_dim(value, (group ^ m) * width, width, dim) for m in (0, 1, 3, 2)],
        axis=dim,
    )


def reduce_groups(send_a, send_b, keep_a, keep_b):
    rows = keep_a.shape[1]

    def exchange(sent, kept, outer, inner):
        got = swap_groups(sent, outer).astype(jnp.float32)
        last = swap_groups((kept[1] + got[rows:]).astype(jnp.bfloat16), inner)
        return kept[0] + got[:rows] + last.astype(jnp.float32)

    return jnp.concatenate([exchange(send_a, keep_a, 3, 1), exchange(send_b, keep_b, 1, 3)], axis=0)


def interleave(first, second, rows):
    width = first.shape[1]
    both = jnp.stack([first.reshape(-1, rows, width), second.reshape(-1, rows, width)], axis=1)
    return both.reshape(-1, width)


def shards(
    buffer, row_ids, enc_weight, dec_weight, threshold_codes, dead_mask, enc_second, dec_second
):
    micros, rows = row_ids.shape
    token_total = micros * rows * 128
    group = lax.axis_index("x")
    thresh = code_step * threshold_codes.astype(jnp.float32)
    dead_flags = dead_mask.astype(jnp.float32)
    enc = own_quarter_first(enc_weight, 0, group)
    dec = own_quarter_first(dec_weight, 1, group)
    own = jnp.stack([own_quarter_first(buffer[row_ids[m]], 1, group) for m in range(micros)])
    tokens = [(mine, swap_cores(mine)) for mine in gather_stages(own)]

    def forward(block):
        preact = jnp.dot(block, enc, preferred_element_type=jnp.float32)
        gating = jax.nn.sigmoid((preact - thresh) / gate_width)
        active = (preact * gating).astype(jnp.bfloat16)
        ghost_act = (jnp.exp(preact) * dead_flags).astype(jnp.bfloat16)
        partial = jnp.dot(
            interleave(active, ghost_act, rows), dec, preferred_element_type=jnp.float32
        ).astype(jnp.bfloat16)
        return preact, partial

    theirs = [forward(tokens[m][1]) for m in range(micros)]
    got = [swap_cores(t[1]) for t in theirs]
    mine = [forward(tokens[m][0]) for m in range(micros)]
    preacts = [mine[0][0], theirs[0][0], mine[1][0], theirs[1][0]]
    summed = reduce_stages([m[1] for m in mine], got)
    shares = []
    for m in range(micros):
        residual = own[m].astype(jnp.float32) - summed[m][:rows]
        ghost = summed[m][rows:]
        rr = jnp.sum(residual * residual, axis=1, keepdims=True)
        gg = jnp.sum(ghost * ghost, axis=1, keepdims=True)
        rg = jnp.sum(residual * ghost, axis=1, keepdims=True)
        scale = jnp.sqrt(rr + norm_eps) / (2.0 * jnp.sqrt(gg + norm_eps))
        cross = jnp.where(scale > 0.0, scale * (scale * gg - 2.0 * rg), 0.0)
        columns = in_parts(scale) + in_parts(rr) + in_parts(rr + cross)
        columns = jnp.concatenate(columns, axis=1)
        columns = jnp.pad(columns, ((0, rows), (0, EXTRA - columns.shape[1])))
        both = jnp.concatenate([residual, ghost], axis=0)
        shares.append(jnp.concatenate([both, columns], axis=1).astype(jnp.bfloat16))
    width = enc.shape[0]
    mine = gather_stages(jnp.stack(shares))
    theirs = [swap_cores(v) for v in mine]
    sums = jnp.stack([jnp.sum(v[:, width:].astype(jnp.float32), axis=0) for v in mine])
    sums = sums + swap_groups(sums, 1)
    sums = sums + swap_groups(sums, 3)
    sums = sums + swap_cores(sums)
    sums = jnp.stack([jnp.sum(sums[:, 3:6], axis=1), jnp.sum(sums[:, 6:9], axis=1)])

    boths = [mine[0], theirs[0], mine[1], theirs[1]]
    backs = [back_project(b, dec) for b in boths]
    pre_grads, dec_pieces = dec_grads(
        rows, sums, thresh.reshape(1, -1), dead_flags.reshape(1, -1), preacts, backs, boths
    )
    enc_pieces = enc_grads(pre_grads, [tokens[m][side] for m in range(micros) for side in range(2)])
    factor = -2.0 / token_total
    dec_grad = reduce_groups(*dec_pieces) * factor
    enc_grad = (reduce_groups(*enc_pieces) * factor).T
    dec_update, dec_second_new = adam_second(dec_grad, dec_second)
    enc_update, enc_second_new = adam_second(enc_grad, enc_second)
    losses = sums / token_total
    return (enc_update, enc_second_new, dec_update, dec_second_new, losses)


def solution(mesh):
    finer = Mesh(mesh.devices.reshape(4, 4, 2, 4), AXES)
    in_specs = (
        P(LAT_DP, None),
        P(None, LAT_DP),
        P(None, LAT),
        P(LAT, None),
        P(LAT),
        P(LAT),
        P("x", LAT),
        P(LAT, "x"),
    )
    out_specs = (P("x", LAT), P("x", LAT), P(LAT, "x"), P(LAT, "x"), P())
    return jax.shard_map(
        shards, mesh=finer, in_specs=in_specs, out_specs=out_specs, check_vma=False
    )
```

```python
import jax
import jax.numpy as jnp
from jax import lax
from jax.experimental import pallas as pl
from jax.experimental.pallas import tpu as pltpu
from jax.sharding import Mesh
from jax.sharding import PartitionSpec as P

LAT_X = ("lat", "x")


gate_width = 0.1
code_step = 0.1
norm_eps = 1e-06
beta_two = 0.999
adam_eps = 1e-08
adam_count = 2000

QUADS = [[z * 8 + y * 2 for z in range(4)] for y in range(4)] + [
    [z * 8 + y * 2 + 1 for y in range(4)] for z in range(4)
]
MASKS = ((1, 3), (3, 1))
STAGES = 2
EXTRA = 128


def adam_second(grads, second):
    renewed = beta_two * second + (1.0 - beta_two) * grads * grads
    correction = 1.0 - beta_two**adam_count
    return (grads / (jnp.sqrt(renewed / correction) + adam_eps), renewed)


def contract(left, right, dim):
    return lax.dot_general(
        left, right, (((dim,), (dim,)), ((), ())), preferred_element_type=jnp.float32
    )


def swap_stage(value, stage, micro):
    mask = MASKS[micro][stage]
    pairs = [(i, i ^ (mask * 8 if i % 2 else mask * 2)) for i in range(32)]
    return lax.ppermute(value, "lat", pairs)


def swap_cores(value):
    return lax.ppermute(value, "lat", [(i, i ^ 1) for i in range(32)])


def exchange_quads(value):
    return lax.all_to_all(
        value, "lat", split_axis=0, concat_axis=0, tiled=True, axis_index_groups=QUADS
    )


def swap_groups(value, mask):
    return lax.ppermute(value, "x", [(i, i ^ mask) for i in range(4)])


def gather_stages(value, *others):
    spread = exchange_quads(jnp.broadcast_to(value, (4, *value.shape)))
    blocks = [spread[:, m].reshape(-1, value.shape[2]) for m in range(2)]
    theirs = lax.optimization_barrier([swap_stage(b, 0, m) for m, b in enumerate(blocks)])
    low = [jnp.concatenate([b, t], axis=0) for b, t in zip(blocks, theirs)]
    high = [swap_stage(b, 1, m) for m, b in enumerate(low)]
    other_low = [swap_cores(b) for b in low]
    high, others = lax.optimization_barrier((high, others))
    other_high = [swap_cores(b) for b in high]
    return list(zip(low, high, other_low, other_high)), others


def add_rounded(mine, theirs):
    return (mine.astype(jnp.float32) + theirs.astype(jnp.float32)).astype(jnp.bfloat16)


def reduce_stages(low, high, other_low, other_high):
    sent = [add_rounded(a, b) for a, b in zip(high, other_high)]
    theirs = [swap_stage(v, 1, m) for m, v in enumerate(sent)]
    mine = [add_rounded(a, b) for a, b in zip(low, other_low)]
    theirs = lax.optimization_barrier(theirs)
    half = mine[0].shape[0] // 2
    sent = [add_rounded(a[half:], b[half:]) for a, b in zip(mine, theirs)]
    mine = [add_rounded(a[:half], b[:half]) for a, b in zip(mine, theirs)]
    theirs = lax.optimization_barrier([swap_stage(v, 0, m) for m, v in enumerate(sent)])
    last = [add_rounded(a, b).reshape(4, -1, a.shape[1]) for a, b in zip(mine, theirs)]
    last = exchange_quads(jnp.stack(last, axis=1))
    return jnp.sum(last.astype(jnp.float32), axis=0)


def in_parts(value):
    high = lax.reduce_precision(value, 8, 7)
    middle = lax.reduce_precision(value - high, 8, 7)
    return [high, middle, value - high - middle]


def vmem(count):
    return [pl.BlockSpec(memory_space=pltpu.VMEM)] * count


def write_grads(left, rights, width, send_a, send_b, keep_a, keep_b):
    rows = keep_a.shape[1]
    lanes = width if width % 128 else 128
    step = lanes if 4 * width % (2 * lanes) else 2 * lanes
    for start in range(0, 4 * width, step):
        right = jnp.concatenate([r[:, start : start + step] for r in rights], axis=0)
        grads = jnp.dot(left, right, preferred_element_type=jnp.float32)
        for at in range(0, step, lanes):
            slot, column = divmod(start + at, width)
            columns = slice(column, column + lanes)
            top, bottom = grads[:rows, at : at + lanes], grads[rows:, at : at + lanes]
            if slot < 2:
                keep_a[slot, :, columns] = top
            else:
                send_a[(slot - 2) * rows : (slot - 1) * rows, columns] = top.astype(jnp.bfloat16)
            if slot % 2 == 0:
                keep_b[slot // 2, :, columns] = bottom
            else:
                row = slot // 2 * rows
                send_b[row : row + rows, columns] = bottom.astype(jnp.bfloat16)


def grad_shapes(latents, width):
    return [jax.ShapeDtypeStruct((latents, width), jnp.bfloat16)] * 2 + [
        jax.ShapeDtypeStruct((2, latents // 2, width), jnp.float32)
    ] * 2


def dec_kernel(rows, sums_ref, thresh_ref, dead_ref, *refs):
    preacts, backs, boths = refs[0:2], refs[2:10], refs[10:18]
    pre_grads, outs = refs[18:20], refs[20:]
    latents = thresh_ref.shape[1]
    features = boths[0].shape[1] - EXTRA
    tokens = boths[0].shape[0] // 2
    lefts = []
    for micro in range(2):
        ratio = sums_ref[0, micro] / sums_ref[1, micro]
        for i in range(4):
            at = slice(i * tokens, (i + 1) * tokens)
            both, back = boths[4 * micro + i], backs[4 * micro + i]
            preact = preacts[micro][at, :]
            gating = jax.nn.sigmoid((preact - thresh_ref[...]) / gate_width)
            raised = jnp.exp(preact) * dead_ref[...]
            active = (preact * gating).astype(jnp.bfloat16).astype(jnp.float32)
            ghost_act = raised.astype(jnp.bfloat16).astype(jnp.float32)
            extra = both[:, features:].astype(jnp.float32).reshape(-1, 2, rows, EXTRA)
            extra = extra[:, 0].reshape(-1, EXTRA)
            scale = extra[:, 0:1] + extra[:, 1:2] + extra[:, 2:3]
            back = back[...].reshape(-1, 2, rows, latents)
            from_residual = back[:, 0].reshape(-1, latents)
            from_ghost = back[:, 1].reshape(-1, latents)
            scaled = jnp.where(scale > 0.0, scale * from_ghost, 0.0)
            ghost_back = scale * (scaled - from_residual)
            pre_grad = (
                from_residual * (gating + preact * gating * (1.0 - gating) / gate_width)
                - ratio * ghost_back * raised
            )
            pre_grads[micro][at, :] = pre_grad.astype(jnp.bfloat16)
            weighted = ratio * (scale * ghost_act)
            pair = (active + weighted).reshape(-1, 1, rows, latents)
            other = -(scale * weighted).reshape(-1, 1, rows, latents)
            lefts.append(jnp.concatenate([pair, other], axis=1).reshape(-1, latents))
    left = jnp.concatenate(lefts, axis=0).T.astype(jnp.bfloat16)
    write_grads(left, boths, features // 4, *outs)


def dec_grads(rows, sums, thresh, dead_flags, preacts, backs, boths):
    latents = thresh.shape[1]
    width = (boths[0].shape[1] - EXTRA) // 4
    out_shape = [jax.ShapeDtypeStruct(p.shape, jnp.bfloat16) for p in preacts]
    outs = pl.pallas_call(
        lambda *refs: dec_kernel(rows, *refs),
        out_shape=out_shape + grad_shapes(latents, width),
        in_specs=[pl.BlockSpec(memory_space=pltpu.SMEM)] + vmem(20),
        out_specs=vmem(6),
        compiler_params=pltpu.CompilerParams(vmem_limit_bytes=24 * 1024 * 1024),
        cost_estimate=pl.CostEstimate(
            flops=64 * latents * width * boths[0].shape[0],
            bytes_accessed=16 * boths[0].size + 24 * latents * width,
            transcendentals=0,
        ),
        name="decoder_gradient",
    )(sums, thresh, dead_flags, *preacts, *backs, *boths)
    return outs[:2], outs[2:]


def enc_kernel(*refs):
    left = jnp.concatenate([r[...].astype(jnp.float32).T for r in refs[0:2]], axis=1)
    write_grads(left.astype(jnp.bfloat16), refs[2:4], refs[2].shape[1] // 4, *refs[4:])


def enc_grads(pre_grads, tokens):
    latents = pre_grads[0].shape[1]
    width = tokens[0].shape[1] // 4
    return pl.pallas_call(
        enc_kernel,
        out_shape=grad_shapes(latents, width),
        in_specs=vmem(4),
        out_specs=vmem(4),
        compiler_params=pltpu.CompilerParams(vmem_limit_bytes=16 * 1024 * 1024),
        cost_estimate=pl.CostEstimate(
            flops=16 * latents * width * tokens[0].shape[0],
            bytes_accessed=4 * tokens[0].size + 24 * latents * width,
            transcendentals=0,
        ),
        name="encoder_gradient",
    )(*pre_grads, *tokens)


def own_quarter_first(value, dim, group):
    width = value.shape[dim] // 4
    return jnp.concatenate(
        [lax.dynamic_slice_in_dim(value, (group ^ m) * width, width, dim) for m in (0, 1, 3, 2)],
        axis=dim,
    )


def reduce_groups(send_a, send_b, keep_a, keep_b):
    rows = keep_a.shape[1]

    def exchange(sent, kept, outer, inner):
        got = swap_groups(sent, outer).astype(jnp.float32)
        last = swap_groups((kept[1] + got[rows:]).astype(jnp.bfloat16), inner)
        return kept[0] + got[:rows] + last.astype(jnp.float32)

    return jnp.concatenate([exchange(send_a, keep_a, 3, 1), exchange(send_b, keep_b, 1, 3)], axis=0)


def interleave(first, second, rows):
    width = first.shape[1]
    both = jnp.stack([first.reshape(-1, rows, width), second.reshape(-1, rows, width)], axis=1)
    return both.reshape(-1, width)


def shards(
    buffer, row_ids, enc_weight, dec_weight, threshold_codes, dead_mask, enc_second, dec_second
):
    micros, rows = row_ids.shape
    token_total = micros * rows * 128
    group = lax.axis_index("x")
    thresh = code_step * threshold_codes.astype(jnp.float32)
    dead_flags = dead_mask.astype(jnp.float32)
    enc = own_quarter_first(enc_weight, 0, group)
    dec = own_quarter_first(dec_weight, 1, group)
    dec = jnp.pad(dec, ((0, 0), (0, EXTRA)))
    own = jnp.stack([own_quarter_first(buffer[row_ids[m]], 1, group) for m in range(micros)])
    pieces, (enc, dec) = gather_stages(own, enc, dec)
    tokens = [jnp.concatenate(p, axis=0) for p in pieces]
    width = enc.shape[0]
    half = tokens[0].shape[0] // 4
    preacts = []
    sides = []
    for m in range(micros):
        preact = jnp.dot(tokens[m], enc, preferred_element_type=jnp.float32)
        gating = jax.nn.sigmoid((preact - thresh) / gate_width)
        active = (preact * gating).astype(jnp.bfloat16)
        ghost_act = (jnp.exp(preact) * dead_flags).astype(jnp.bfloat16)
        preacts.append(preact)
        sides.append(interleave(active, ghost_act, rows))

    def rebuild(block, m):
        left = sides[m][2 * half * block : 2 * half * (block + 1)]
        out = jnp.dot(left, dec[:, :width], preferred_element_type=jnp.float32)
        return out.astype(jnp.bfloat16)

    other_high = [swap_cores(rebuild(3, m)) for m in range(micros)]
    other_low = [swap_cores(rebuild(2, m)) for m in range(micros)]
    high = [rebuild(1, m) for m in range(micros)]
    low = [rebuild(0, m) for m in range(micros)]
    summed = reduce_stages(low, high, other_low, other_high)
    shares = []
    for m in range(micros):
        residual = own[m].astype(jnp.float32) - summed[m][:rows]
        ghost = summed[m][rows:]
        rr = jnp.sum(residual * residual, axis=1, keepdims=True)
        gg = jnp.sum(ghost * ghost, axis=1, keepdims=True)
        rg = jnp.sum(residual * ghost, axis=1, keepdims=True)
        scale = jnp.sqrt(rr + norm_eps) / (2.0 * jnp.sqrt(gg + norm_eps))
        cross = jnp.where(scale > 0.0, scale * (scale * gg - 2.0 * rg), 0.0)
        columns = in_parts(scale) + in_parts(rr) + in_parts(rr + cross)
        columns = jnp.concatenate(columns, axis=1)
        columns = jnp.pad(columns, ((0, rows), (0, EXTRA - columns.shape[1])))
        both = jnp.concatenate([residual, ghost], axis=0)
        shares.append(jnp.concatenate([both, columns], axis=1).astype(jnp.bfloat16))
    gathered, _ = gather_stages(jnp.stack(shares))
    sums = jnp.stack(
        [
            jnp.sum(low[:, width:].astype(jnp.float32) + high[:, width:].astype(jnp.float32), axis=0)
            for low, high, _, _ in gathered
        ]
    )
    sums = sums + swap_groups(sums, 1)
    sums = sums + swap_groups(sums, 3)
    sums = sums + swap_cores(sums)
    sums = jnp.stack([jnp.sum(sums[:, 3:6], axis=1), jnp.sum(sums[:, 6:9], axis=1)])

    boths = [block for blocks in gathered for block in blocks]
    backs = [contract(block, dec, 1) for block in boths]
    pre_grads, dec_pieces = dec_grads(
        rows, sums, thresh.reshape(1, -1), dead_flags.reshape(1, -1), preacts, backs, boths
    )
    enc_pieces = enc_grads(pre_grads, tokens)
    factor = -2.0 / token_total
    dec_grad = reduce_groups(*dec_pieces) * factor
    enc_grad = (reduce_groups(*enc_pieces) * factor).T
    dec_update, dec_second_new = adam_second(dec_grad, dec_second)
    enc_update, enc_second_new = adam_second(enc_grad, enc_second)
    losses = sums / token_total
    return (enc_update, enc_second_new, dec_update, dec_second_new, losses)


def solution(mesh):
    renamed = Mesh(mesh.devices, LAT_X)
    in_specs = (
        P(LAT_X, None),
        P(None, LAT_X),
        P(None, "lat"),
        P("lat", None),
        P("lat"),
        P("lat"),
        P("x", "lat"),
        P("lat", "x"),
    )
    out_specs = (P("x", "lat"), P("x", "lat"), P("lat", "x"), P("lat", "x"), P())
    return jax.shard_map(
        shards, mesh=renamed, in_specs=in_specs, out_specs=out_specs, check_vma=False
    )
```

```python
import jax
import jax.numpy as jnp
from jax import lax
from jax.experimental import pallas as pl
from jax.experimental.pallas import tpu as pltpu
from jax.sharding import Mesh
from jax.sharding import PartitionSpec as P

LAT_X = ("lat", "x")


gate_width = 0.1
code_step = 0.1
norm_eps = 1e-06
beta_two = 0.999
adam_eps = 1e-08
adam_count = 2000

QUAD_MASKS = (1, 3, 2)
MASKS = ((1, 3), (3, 1))
STAGES = 2
EXTRA = 128


def adam_second(grads, second):
    renewed = beta_two * second + (1.0 - beta_two) * grads * grads
    correction = 1.0 - beta_two**adam_count
    return (grads / (jnp.sqrt(renewed / correction) + adam_eps), renewed)


def contract(left, right, dim):
    return lax.dot_general(
        left, right, (((dim,), (dim,)), ((), ())), preferred_element_type=jnp.float32
    )


def swap_stage(value, stage, micro):
    mask = MASKS[micro][stage]
    pairs = [(i, i ^ (mask * 8 if i % 2 else mask * 2)) for i in range(32)]
    return lax.ppermute(value, "lat", pairs)


def swap_cores(value):
    return lax.ppermute(value, "lat", [(i, i ^ 1) for i in range(32)])


def exchange_quads(values, crossed=False):
    step = (2, 8) if crossed else (8, 2)
    return [
        lax.ppermute(v, "lat", [(i, i ^ (mask * step[i % 2])) for i in range(32)])
        for v, mask in zip(values, QUAD_MASKS)
    ]


def swap_opposite(value):
    return lax.ppermute(value, "lat", [(i, i ^ (2 * (8 if i % 2 else 2))) for i in range(32)])


def swap_groups(value, mask):
    return lax.ppermute(value, "x", [(i, i ^ mask) for i in range(4)])


def gather_tokens(value, *others):
    spread = [value] + lax.optimization_barrier(exchange_quads([value] * 3))
    block = jnp.concatenate(spread, axis=1)
    near = exchange_quads([block] * 3, crossed=True)
    first = swap_cores(block)
    near, others = lax.optimization_barrier((near, others))
    mine = [block] + near
    theirs = [first] + [swap_cores(v) for v in near]
    tokens = []
    for m in range(2):
        order = [0] + [1 + QUAD_MASKS.index(k) for k in (MASKS[m][0], MASKS[m][1], 2)]
        tokens.append(jnp.concatenate([side[k][m] for side in (mine, theirs) for k in order], axis=0))
    return tokens, others


def gather_stages(value):
    spread = [value] + lax.optimization_barrier(exchange_quads([value] * 3))
    blocks = [jnp.concatenate([v[m] for v in spread], axis=0) for m in range(2)]
    theirs = lax.optimization_barrier([swap_stage(b, 0, m) for m, b in enumerate(blocks)])
    low = [jnp.concatenate([b, t], axis=0) for b, t in zip(blocks, theirs)]
    high = [swap_stage(b, 1, m) for m, b in enumerate(low)]
    return low, [swap_cores(b) for b in low], high


def add_rounded(mine, theirs):
    return (mine.astype(jnp.float32) + theirs.astype(jnp.float32)).astype(jnp.bfloat16)


def reduce_stages(low, high, other_low, other_high):
    sent = [add_rounded(a, b) for a, b in zip(high, other_high)]
    theirs = [swap_stage(v, 1, m) for m, v in enumerate(sent)]
    mine = [add_rounded(a, b) for a, b in zip(low, other_low)]
    theirs = lax.optimization_barrier(theirs)
    half = mine[0].shape[0] // 2
    sent = [add_rounded(a[half:], b[half:]) for a, b in zip(mine, theirs)]
    mine = [add_rounded(a[:half], b[:half]) for a, b in zip(mine, theirs)]
    theirs = lax.optimization_barrier([swap_stage(v, 0, m) for m, v in enumerate(sent)])
    last = [add_rounded(a, b).reshape(4, -1, a.shape[1]) for a, b in zip(mine, theirs)]
    sent = [jnp.stack([v[k] for v in last]) for k in range(4)]
    got = lax.optimization_barrier(exchange_quads(sent[1:]))
    return sum((v.astype(jnp.float32) for v in got), sent[0].astype(jnp.float32))


def in_parts(value):
    high = lax.reduce_precision(value, 8, 7)
    middle = lax.reduce_precision(value - high, 8, 7)
    return [high, middle, value - high - middle]


def vmem(count):
    return [pl.BlockSpec(memory_space=pltpu.VMEM)] * count


def write_grads(left, rights, width, send_a, send_b, keep_a, keep_b):
    rows = keep_a.shape[1]
    lanes = width if width % 128 else 128
    step = lanes if 4 * width % (2 * lanes) else 2 * lanes
    for start in range(0, 4 * width, step):
        right = jnp.concatenate([r[:, start : start + step] for r in rights], axis=0)
        grads = jnp.dot(left, right, preferred_element_type=jnp.float32)
        for at in range(0, step, lanes):
            slot, column = divmod(start + at, width)
            columns = slice(column, column + lanes)
            top, bottom = grads[:rows, at : at + lanes], grads[rows:, at : at + lanes]
            if slot < 2:
                keep_a[slot, :, columns] = top
            else:
                send_a[(slot - 2) * rows : (slot - 1) * rows, columns] = top.astype(jnp.bfloat16)
            if slot % 2 == 0:
                keep_b[slot // 2, :, columns] = bottom
            else:
                row = slot // 2 * rows
                send_b[row : row + rows, columns] = bottom.astype(jnp.bfloat16)


def grad_shapes(latents, width):
    return [jax.ShapeDtypeStruct((latents, width), jnp.bfloat16)] * 2 + [
        jax.ShapeDtypeStruct((2, latents // 2, width), jnp.float32)
    ] * 2


def dec_kernel(rows, sums_ref, thresh_ref, dead_ref, *refs):
    preacts, backs, boths = refs[0:2], refs[2:10], refs[10:18]
    pre_grads, outs = refs[18:20], refs[20:]
    latents = thresh_ref.shape[1]
    features = boths[0].shape[1] - EXTRA
    tokens = boths[0].shape[0] // 2
    lefts = []
    for micro in range(2):
        ratio = sums_ref[0, micro] / sums_ref[1, micro]
        for i in range(4):
            at = slice(i * tokens, (i + 1) * tokens)
            both, back = boths[4 * micro + i], backs[4 * micro + i]
            preact = preacts[micro][at, :]
            gating = jax.nn.sigmoid((preact - thresh_ref[...]) / gate_width)
            raised = jnp.exp(preact) * dead_ref[...]
            active = (preact * gating).astype(jnp.bfloat16).astype(jnp.float32)
            ghost_act = raised.astype(jnp.bfloat16).astype(jnp.float32)
            extra = both[:, features:].astype(jnp.float32).reshape(-1, 2, rows, EXTRA)
            extra = extra[:, 0].reshape(-1, EXTRA)
            scale = extra[:, 0:1] + extra[:, 1:2] + extra[:, 2:3]
            back = back[...].reshape(-1, 2, rows, latents)
            from_residual = back[:, 0].reshape(-1, latents)
            from_ghost = back[:, 1].reshape(-1, latents)
            scaled = jnp.where(scale > 0.0, scale * from_ghost, 0.0)
            ghost_back = scale * (scaled - from_residual)
            pre_grad = (
                from_residual * (gating + preact * gating * (1.0 - gating) / gate_width)
                - ratio * ghost_back * raised
            )
            pre_grads[micro][at, :] = pre_grad.astype(jnp.bfloat16)
            weighted = ratio * (scale * ghost_act)
            pair = (active + weighted).reshape(-1, 1, rows, latents)
            other = -(scale * weighted).reshape(-1, 1, rows, latents)
            lefts.append(jnp.concatenate([pair, other], axis=1).reshape(-1, latents))
    left = jnp.concatenate(lefts, axis=0).T.astype(jnp.bfloat16)
    write_grads(left, boths, features // 4, *outs)


def dec_grads(rows, sums, thresh, dead_flags, preacts, backs, boths):
    latents = thresh.shape[1]
    width = (boths[0].shape[1] - EXTRA) // 4
    out_shape = [jax.ShapeDtypeStruct(p.shape, jnp.bfloat16) for p in preacts]
    outs = pl.pallas_call(
        lambda *refs: dec_kernel(rows, *refs),
        out_shape=out_shape + grad_shapes(latents, width),
        in_specs=[pl.BlockSpec(memory_space=pltpu.SMEM)] + vmem(20),
        out_specs=vmem(6),
        compiler_params=pltpu.CompilerParams(vmem_limit_bytes=24 * 1024 * 1024),
        cost_estimate=pl.CostEstimate(
            flops=64 * latents * width * boths[0].shape[0],
            bytes_accessed=16 * boths[0].size + 24 * latents * width,
            transcendentals=0,
        ),
        name="decoder_gradient",
    )(sums, thresh, dead_flags, *preacts, *backs, *boths)
    return outs[:2], outs[2:]


def enc_kernel(*refs):
    left = jnp.concatenate([r[...].astype(jnp.float32).T for r in refs[0:2]], axis=1)
    write_grads(left.astype(jnp.bfloat16), refs[2:4], refs[2].shape[1] // 4, *refs[4:])


def enc_grads(pre_grads, tokens):
    latents = pre_grads[0].shape[1]
    width = tokens[0].shape[1] // 4
    return pl.pallas_call(
        enc_kernel,
        out_shape=grad_shapes(latents, width),
        in_specs=vmem(4),
        out_specs=vmem(4),
        compiler_params=pltpu.CompilerParams(vmem_limit_bytes=16 * 1024 * 1024),
        cost_estimate=pl.CostEstimate(
            flops=16 * latents * width * tokens[0].shape[0],
            bytes_accessed=4 * tokens[0].size + 24 * latents * width,
            transcendentals=0,
        ),
        name="encoder_gradient",
    )(*pre_grads, *tokens)


def own_quarter_first(value, dim, group):
    width = value.shape[dim] // 4
    return jnp.concatenate(
        [lax.dynamic_slice_in_dim(value, (group ^ m) * width, width, dim) for m in (0, 1, 3, 2)],
        axis=dim,
    )


def reduce_groups(dec_pieces, enc_pieces):
    rows = dec_pieces[2].shape[1]

    def first(send_a, send_b, keep_a, keep_b):
        return [swap_groups(send_a, 3), swap_groups(send_b, 1)]

    def middle(got, pieces):
        return [
            (kept[1] + half[rows:].astype(jnp.float32)).astype(jnp.bfloat16)
            for half, kept in zip(got, pieces[2:])
        ]

    def last(sent):
        return [swap_groups(sent[0], 1), swap_groups(sent[1], 3)]

    def parts(pieces, got, end):
        return [v for i in range(2) for v in (pieces[2 + i], got[i], end[i])]

    dec_got, enc_got = first(*dec_pieces), first(*enc_pieces)
    dec_sent = middle(dec_got, dec_pieces)
    dec_end = last(dec_sent)
    enc_got, _ = lax.optimization_barrier((enc_got, dec_sent))
    enc_end = last(middle(enc_got, enc_pieces))
    return parts(dec_pieces, dec_got, dec_end), parts(enc_pieces, enc_got, enc_end)


def update_kernel(factor, turned, *refs):
    keep_a, got_a, last_a, keep_b, got_b, last_b, second_ref = refs[0:7]
    update_out, renewed_out, update_ref, renewed_ref, sems = refs[7:]
    rows, width = last_a.shape

    def total(keep, got, last, at):
        first = slice(at[0].start, at[0].stop)
        return keep[0, first, at[1]] + (
            got[first, at[1]].astype(jnp.float32) + last[first, at[1]].astype(jnp.float32)
        )

    copies = []
    count = sems.shape[1]
    size = second_ref.shape[0] // count
    for i in range(count):
        block = slice(i * size, (i + 1) * size)
        if turned:
            at = (slice(0, rows), block)
            grads = jnp.concatenate(
                [total(keep_a, got_a, last_a, at), total(keep_b, got_b, last_b, at)], axis=0
            ).T
        else:
            start = i * size % rows
            at = (slice(start, start + size), slice(0, width))
            half = (keep_a, got_a, last_a) if i * size < rows else (keep_b, got_b, last_b)
            grads = total(*half, at)
        values = adam_second(grads * factor, second_ref[block, :])
        for k, (value, ref, out) in enumerate(
            zip(values, (update_ref, renewed_ref), (update_out, renewed_out))
        ):
            ref[block, :] = value
            copy = pltpu.make_async_copy(ref.at[block, :], out.at[block, :], sems.at[k, i])
            copy.start()
            copies.append(copy)
    for copy in copies:
        copy.wait()


def update(parts, second, factor, turned):
    count = (7 if second.shape[0] % 896 == 0 else 1) if turned else 4
    return pl.pallas_call(
        lambda *refs: update_kernel(factor, turned, *refs),
        out_shape=[jax.ShapeDtypeStruct(second.shape, jnp.float32)] * 2,
        in_specs=vmem(7),
        out_specs=[pl.BlockSpec(memory_space=pl.ANY)] * 2,
        scratch_shapes=[
            pltpu.VMEM(second.shape, jnp.float32),
            pltpu.VMEM(second.shape, jnp.float32),
            pltpu.SemaphoreType.DMA((2, count)),
        ],
        compiler_params=pltpu.CompilerParams(vmem_limit_bytes=12 * 1024 * 1024),
        cost_estimate=pl.CostEstimate(
            flops=20 * second.size, bytes_accessed=20 * second.size, transcendentals=second.size
        ),
        name="encoder_update" if turned else "decoder_update",
    )(*parts, second)


def interleave(first, second, rows):
    width = first.shape[1]
    both = jnp.stack([first.reshape(-1, rows, width), second.reshape(-1, rows, width)], axis=1)
    return both.reshape(-1, width)


def shards(
    buffer, row_ids, enc_weight, dec_weight, threshold_codes, dead_mask, enc_second, dec_second
):
    micros, rows = row_ids.shape
    token_total = micros * rows * 128
    group = lax.axis_index("x")
    thresh = code_step * threshold_codes.astype(jnp.float32)
    dead_flags = dead_mask.astype(jnp.float32)
    enc = own_quarter_first(enc_weight, 0, group)
    dec = own_quarter_first(dec_weight, 1, group)
    dec = jnp.pad(dec, ((0, 0), (0, EXTRA)))
    own = jnp.stack([own_quarter_first(buffer[row_ids[m]], 1, group) for m in range(micros)])
    tokens, (enc, dec) = gather_tokens(own, enc, dec)
    width = enc.shape[0]
    half = tokens[0].shape[0] // 4
    preacts = []
    sides = []
    for m in range(micros):
        preact = jnp.dot(tokens[m], enc, preferred_element_type=jnp.float32)
        gating = jax.nn.sigmoid((preact - thresh) / gate_width)
        active = (preact * gating).astype(jnp.bfloat16)
        ghost_act = (jnp.exp(preact) * dead_flags).astype(jnp.bfloat16)
        preacts.append(preact)
        sides.append(interleave(active, ghost_act, rows))

    def rebuild(block, m):
        left = sides[m][2 * half * block : 2 * half * (block + 1)]
        out = jnp.dot(left, dec[:, :width], preferred_element_type=jnp.float32)
        return out.astype(jnp.bfloat16)

    other_high = [swap_cores(rebuild(3, m)) for m in range(micros)]
    other_low = [swap_cores(rebuild(2, m)) for m in range(micros)]
    high = [rebuild(1, m) for m in range(micros)]
    low = [rebuild(0, m) for m in range(micros)]
    summed = reduce_stages(low, high, other_low, other_high)
    shares = []
    for m in range(micros):
        residual = own[m].astype(jnp.float32) - summed[m][:rows]
        ghost = summed[m][rows:]
        rr = jnp.sum(residual * residual, axis=1, keepdims=True)
        gg = jnp.sum(ghost * ghost, axis=1, keepdims=True)
        rg = jnp.sum(residual * ghost, axis=1, keepdims=True)
        scale = jnp.sqrt(rr + norm_eps) / (2.0 * jnp.sqrt(gg + norm_eps))
        cross = jnp.where(scale > 0.0, scale * (scale * gg - 2.0 * rg), 0.0)
        columns = in_parts(scale) + in_parts(rr) + in_parts(rr + cross)
        columns = jnp.concatenate(columns, axis=1)
        columns = jnp.pad(columns, ((0, rows), (0, EXTRA - columns.shape[1])))
        both = jnp.concatenate([residual, ghost], axis=0)
        shares.append(jnp.concatenate([both, columns], axis=1).astype(jnp.bfloat16))
    low, other_low, high = gather_stages(jnp.stack(shares))
    sums = jnp.stack([jnp.sum(b[:, width:].astype(jnp.float32), axis=0) for b in low])
    sums, other_low = lax.optimization_barrier((sums, other_low))
    sums = sums + swap_groups(sums, 1)
    sums = sums + swap_groups(sums, 3)
    sums = sums + swap_opposite(sums)
    early = [contract(block, dec, 1) for block in low + other_low]
    high, early, sums = lax.optimization_barrier((high, early, sums))
    sums = sums + swap_cores(sums)
    sums = jnp.stack([jnp.sum(sums[:, 3:6], axis=1), jnp.sum(sums[:, 6:9], axis=1)])
    other_high = [swap_cores(b) for b in high]
    late = [contract(block, dec, 1) for block in high + other_high]
    boths = [b[m] for m in range(micros) for b in (low, high, other_low, other_high)]
    backs = [b[i + m] for m in range(micros) for i in (0, 2) for b in (early, late)]
    pre_grads, dec_pieces = dec_grads(
        rows, sums, thresh.reshape(1, -1), dead_flags.reshape(1, -1), preacts, backs, boths
    )
    enc_pieces = enc_grads(pre_grads, tokens)
    factor = -2.0 / token_total
    dec_parts, enc_parts = reduce_groups(dec_pieces, enc_pieces)
    decoder = update(dec_parts, dec_second, factor, False)
    (enc_parts[2], enc_parts[5]), decoder = lax.optimization_barrier(
        ((enc_parts[2], enc_parts[5]), decoder)
    )
    dec_update, dec_second_new = decoder
    enc_update, enc_second_new = update(enc_parts, enc_second, factor, True)
    losses = sums / token_total
    return (enc_update, enc_second_new, dec_update, dec_second_new, losses)


def solution(mesh):
    renamed = Mesh(mesh.devices, LAT_X)
    in_specs = (
        P(LAT_X, None),
        P(None, LAT_X),
        P(None, "lat"),
        P("lat", None),
        P("lat"),
        P("lat"),
        P("x", "lat"),
        P("lat", "x"),
    )
    out_specs = (P("x", "lat"), P("x", "lat"), P("lat", "x"), P("lat", "x"), P())
    return jax.shard_map(
        shards, mesh=renamed, in_specs=in_specs, out_specs=out_specs, check_vma=False
    )
```

```python
import jax
import jax.numpy as jnp
from jax import lax
from jax.experimental import pallas as pl
from jax.experimental.pallas import tpu as pltpu
from jax.sharding import Mesh
from jax.sharding import PartitionSpec as P

LAT_X = ("lat", "x")


gate_width = 0.1
code_step = 0.1
norm_eps = 1e-06
beta_two = 0.999
adam_eps = 1e-08
adam_count = 2000

QUAD_MASKS = (1, 3, 2)
MASKS = ((1, 3), (3, 1))
STAGES = 2
EXTRA = 128


def adam_second(grads, second):
    renewed = beta_two * second + (1.0 - beta_two) * grads * grads
    correction = 1.0 - beta_two**adam_count
    return (grads / (jnp.sqrt(renewed / correction) + adam_eps), renewed)


def contract(left, right, dim):
    return lax.dot_general(
        left, right, (((dim,), (dim,)), ((), ())), preferred_element_type=jnp.float32
    )


def swap_stage(value, stage, micro):
    mask = MASKS[micro][stage]
    pairs = [(i, i ^ (mask * 8 if i % 2 else mask * 2)) for i in range(32)]
    return lax.ppermute(value, "lat", pairs)


def swap_cores(value):
    return lax.ppermute(value, "lat", [(i, i ^ 1) for i in range(32)])


def exchange_quads(values, crossed=False):
    step = (2, 8) if crossed else (8, 2)
    return [
        lax.ppermute(v, "lat", [(i, i ^ (mask * step[i % 2])) for i in range(32)])
        for v, mask in zip(values, QUAD_MASKS)
    ]


def swap_opposite(value):
    return lax.ppermute(value, "lat", [(i, i ^ (2 * (8 if i % 2 else 2))) for i in range(32)])


def swap_groups(value, mask):
    return lax.ppermute(value, "x", [(i, i ^ mask) for i in range(4)])


def gather_tokens(value, *others):
    spread = [value] + lax.optimization_barrier(exchange_quads([value] * 3))
    block = jnp.concatenate(spread, axis=1)
    near = exchange_quads([block] * 3, crossed=True)
    first = swap_cores(block)
    near, others = lax.optimization_barrier((near, others))
    mine = [block] + near
    theirs = [first] + [swap_cores(v) for v in near]
    tokens = []
    for m in range(2):
        order = [0] + [1 + QUAD_MASKS.index(k) for k in (MASKS[m][0], MASKS[m][1], 2)]
        tokens.append(jnp.concatenate([side[k][m] for side in (mine, theirs) for k in order], axis=0))
    return tokens, others


def gather_stages(value):
    spread = [value] + lax.optimization_barrier(exchange_quads([value] * 3))
    blocks = [jnp.concatenate([v[m] for v in spread], axis=0) for m in range(2)]
    theirs = lax.optimization_barrier([swap_stage(b, 0, m) for m, b in enumerate(blocks)])
    low = [jnp.concatenate([b, t], axis=0) for b, t in zip(blocks, theirs)]
    high = [swap_stage(b, 1, m) for m, b in enumerate(low)]
    return low, [swap_cores(b) for b in low], high


def add_rounded(mine, theirs):
    return (mine.astype(jnp.float32) + theirs.astype(jnp.float32)).astype(jnp.bfloat16)


def reduce_stages(low, high, other_low, other_high):
    sent = [add_rounded(a, b) for a, b in zip(high, other_high)]
    theirs = [swap_stage(v, 1, m) for m, v in enumerate(sent)]
    mine = [add_rounded(a, b) for a, b in zip(low, other_low)]
    half = mine[0].shape[0] // 2
    sent = [add_rounded(a[half:], b[half:]) for a, b in zip(mine, theirs)]
    mine = [add_rounded(a[:half], b[:half]) for a, b in zip(mine, theirs)]
    theirs = [swap_stage(v, 0, m) for m, v in enumerate(sent)]
    last = [add_rounded(a, b).reshape(4, -1, a.shape[1]) for a, b in zip(mine, theirs)]
    sent = [jnp.stack([v[k] for v in last]) for k in range(4)]
    got = lax.optimization_barrier(exchange_quads(sent[1:]))
    return sum((v.astype(jnp.float32) for v in got), sent[0].astype(jnp.float32))


def in_parts(value):
    high = lax.reduce_precision(value, 8, 7)
    middle = lax.reduce_precision(value - high, 8, 7)
    return [high, middle, value - high - middle]


def vmem(count):
    return [pl.BlockSpec(memory_space=pltpu.VMEM)] * count


def write_grads(left, rights, width, send_a, send_b, keep_a, keep_b):
    rows = keep_a.shape[1]
    lanes = width if width % 128 else 128
    step = lanes if 4 * width % (2 * lanes) else 2 * lanes
    for start in range(0, 4 * width, step):
        right = jnp.concatenate([r[:, start : start + step] for r in rights], axis=0)
        grads = jnp.dot(left, right, preferred_element_type=jnp.float32)
        for at in range(0, step, lanes):
            slot, column = divmod(start + at, width)
            columns = slice(column, column + lanes)
            top, bottom = grads[:rows, at : at + lanes], grads[rows:, at : at + lanes]
            if slot < 2:
                keep_a[slot, :, columns] = top
            else:
                send_a[(slot - 2) * rows : (slot - 1) * rows, columns] = top.astype(jnp.bfloat16)
            if slot % 2 == 0:
                keep_b[slot // 2, :, columns] = bottom
            else:
                row = slot // 2 * rows
                send_b[row : row + rows, columns] = bottom.astype(jnp.bfloat16)


def grad_shapes(latents, width):
    return [jax.ShapeDtypeStruct((latents, width), jnp.bfloat16)] * 2 + [
        jax.ShapeDtypeStruct((2, latents // 2, width), jnp.float32)
    ] * 2


def dec_kernel(rows, sums_ref, thresh_ref, dead_ref, *refs):
    preacts, backs, boths = refs[0:2], refs[2:10], refs[10:18]
    pre_grads, outs = refs[18:20], refs[20:]
    latents = thresh_ref.shape[1]
    features = boths[0].shape[1] - EXTRA
    tokens = boths[0].shape[0] // 2
    lefts = []
    for micro in range(2):
        ratio = sums_ref[0, micro] / sums_ref[1, micro]
        for i in range(4):
            at = slice(i * tokens, (i + 1) * tokens)
            both, back = boths[4 * micro + i], backs[4 * micro + i]
            preact = preacts[micro][at, :]
            gating = jax.nn.sigmoid((preact - thresh_ref[...]) / gate_width)
            raised = jnp.exp(preact) * dead_ref[...]
            active = (preact * gating).astype(jnp.bfloat16).astype(jnp.float32)
            ghost_act = raised.astype(jnp.bfloat16).astype(jnp.float32)
            extra = both[:, features:].astype(jnp.float32).reshape(-1, 2, rows, EXTRA)
            extra = extra[:, 0].reshape(-1, EXTRA)
            scale = extra[:, 0:1] + extra[:, 1:2] + extra[:, 2:3]
            back = back[...].reshape(-1, 2, rows, latents)
            from_residual = back[:, 0].reshape(-1, latents)
            from_ghost = back[:, 1].reshape(-1, latents)
            scaled = jnp.where(scale > 0.0, scale * from_ghost, 0.0)
            ghost_back = scale * (scaled - from_residual)
            pre_grad = (
                from_residual * (gating + preact * gating * (1.0 - gating) / gate_width)
                - ratio * ghost_back * raised
            )
            pre_grads[micro][at, :] = pre_grad.astype(jnp.bfloat16)
            weighted = ratio * (scale * ghost_act)
            pair = (active + weighted).reshape(-1, 1, rows, latents)
            other = -(scale * weighted).reshape(-1, 1, rows, latents)
            lefts.append(jnp.concatenate([pair, other], axis=1).reshape(-1, latents))
    left = jnp.concatenate(lefts, axis=0).T.astype(jnp.bfloat16)
    write_grads(left, boths, features // 4, *outs)


def dec_grads(rows, sums, thresh, dead_flags, preacts, backs, boths):
    latents = thresh.shape[1]
    width = (boths[0].shape[1] - EXTRA) // 4
    out_shape = [jax.ShapeDtypeStruct(p.shape, jnp.bfloat16) for p in preacts]
    outs = pl.pallas_call(
        lambda *refs: dec_kernel(rows, *refs),
        out_shape=out_shape + grad_shapes(latents, width),
        in_specs=[pl.BlockSpec(memory_space=pltpu.SMEM)] + vmem(20),
        out_specs=vmem(6),
        compiler_params=pltpu.CompilerParams(vmem_limit_bytes=24 * 1024 * 1024),
        cost_estimate=pl.CostEstimate(
            flops=64 * latents * width * boths[0].shape[0],
            bytes_accessed=16 * boths[0].size + 24 * latents * width,
            transcendentals=0,
        ),
        name="decoder_gradient",
    )(sums, thresh, dead_flags, *preacts, *backs, *boths)
    return outs[:2], outs[2:]


def enc_kernel(*refs):
    left = jnp.concatenate([r[...].astype(jnp.float32).T for r in refs[0:2]], axis=1)
    write_grads(left.astype(jnp.bfloat16), refs[2:4], refs[2].shape[1] // 4, *refs[4:])


def enc_grads(pre_grads, tokens):
    latents = pre_grads[0].shape[1]
    width = tokens[0].shape[1] // 4
    return pl.pallas_call(
        enc_kernel,
        out_shape=grad_shapes(latents, width),
        in_specs=vmem(4),
        out_specs=vmem(4),
        compiler_params=pltpu.CompilerParams(vmem_limit_bytes=16 * 1024 * 1024),
        cost_estimate=pl.CostEstimate(
            flops=16 * latents * width * tokens[0].shape[0],
            bytes_accessed=4 * tokens[0].size + 24 * latents * width,
            transcendentals=0,
        ),
        name="encoder_gradient",
    )(*pre_grads, *tokens)


def own_quarter_first(value, dim, group):
    width = value.shape[dim] // 4
    return jnp.concatenate(
        [lax.dynamic_slice_in_dim(value, (group ^ m) * width, width, dim) for m in (0, 1, 3, 2)],
        axis=dim,
    )


def reduce_groups(dec_pieces, enc_pieces):
    rows = dec_pieces[2].shape[1]

    def first(send_a, send_b, keep_a, keep_b):
        return [swap_groups(send_a, 3), swap_groups(send_b, 1)]

    def middle(got, pieces):
        return [
            (kept[1] + half[rows:].astype(jnp.float32)).astype(jnp.bfloat16)
            for half, kept in zip(got, pieces[2:])
        ]

    def last(sent):
        return [swap_groups(sent[0], 1), swap_groups(sent[1], 3)]

    def parts(pieces, got, end):
        return [v for i in range(2) for v in (pieces[2 + i], got[i], end[i])]

    dec_got, enc_got = first(*dec_pieces), first(*enc_pieces)
    dec_sent = middle(dec_got, dec_pieces)
    dec_end = last(dec_sent)
    enc_got, _ = lax.optimization_barrier((enc_got, dec_sent))
    enc_end = last(middle(enc_got, enc_pieces))
    return parts(dec_pieces, dec_got, dec_end), parts(enc_pieces, enc_got, enc_end)


def update_kernel(factor, turned, *refs):
    keep_a, got_a, last_a, keep_b, got_b, last_b, second_ref = refs[0:7]
    update_out, renewed_out, update_ref, renewed_ref, sems = refs[7:]
    rows, width = last_a.shape

    def total(keep, got, last, at):
        first = slice(at[0].start, at[0].stop)
        return keep[0, first, at[1]] + (
            got[first, at[1]].astype(jnp.float32) + last[first, at[1]].astype(jnp.float32)
        )

    copies = []
    count = sems.shape[1]
    size = second_ref.shape[0] // count
    for i in range(count):
        block = slice(i * size, (i + 1) * size)
        if turned:
            at = (slice(0, rows), block)
            grads = jnp.concatenate(
                [total(keep_a, got_a, last_a, at), total(keep_b, got_b, last_b, at)], axis=0
            ).T
        else:
            start = i * size % rows
            at = (slice(start, start + size), slice(0, width))
            half = (keep_a, got_a, last_a) if i * size < rows else (keep_b, got_b, last_b)
            grads = total(*half, at)
        values = adam_second(grads * factor, second_ref[block, :])
        for k, (value, ref, out) in enumerate(
            zip(values, (update_ref, renewed_ref), (update_out, renewed_out))
        ):
            ref[block, :] = value
            copy = pltpu.make_async_copy(ref.at[block, :], out.at[block, :], sems.at[k, i])
            copy.start()
            copies.append(copy)
    for copy in copies:
        copy.wait()


def update(parts, second, factor, turned):
    count = (7 if second.shape[0] % 896 == 0 else 1) if turned else 4
    return pl.pallas_call(
        lambda *refs: update_kernel(factor, turned, *refs),
        out_shape=[jax.ShapeDtypeStruct(second.shape, jnp.float32)] * 2,
        in_specs=vmem(7),
        out_specs=[pl.BlockSpec(memory_space=pl.ANY)] * 2,
        scratch_shapes=[
            pltpu.VMEM(second.shape, jnp.float32),
            pltpu.VMEM(second.shape, jnp.float32),
            pltpu.SemaphoreType.DMA((2, count)),
        ],
        compiler_params=pltpu.CompilerParams(vmem_limit_bytes=12 * 1024 * 1024),
        cost_estimate=pl.CostEstimate(
            flops=20 * second.size, bytes_accessed=20 * second.size, transcendentals=second.size
        ),
        name="encoder_update" if turned else "decoder_update",
    )(*parts, second)


def interleave(first, second, rows):
    width = first.shape[1]
    both = jnp.stack([first.reshape(-1, rows, width), second.reshape(-1, rows, width)], axis=1)
    return both.reshape(-1, width)


def shards(
    buffer, row_ids, enc_weight, dec_weight, threshold_codes, dead_mask, enc_second, dec_second
):
    micros, rows = row_ids.shape
    token_total = micros * rows * 128
    group = lax.axis_index("x")
    thresh = code_step * threshold_codes.astype(jnp.float32)
    dead_flags = dead_mask.astype(jnp.float32)
    enc = own_quarter_first(enc_weight, 0, group)
    dec = own_quarter_first(dec_weight, 1, group)
    dec = jnp.pad(dec, ((0, 0), (0, EXTRA)))
    own = jnp.stack([own_quarter_first(buffer[row_ids[m]], 1, group) for m in range(micros)])
    tokens, (enc, dec) = gather_tokens(own, enc, dec)
    width = enc.shape[0]
    half = tokens[0].shape[0] // 4
    preacts = []
    sides = []
    for m in range(micros):
        preact = jnp.dot(tokens[m], enc, preferred_element_type=jnp.float32)
        gating = jax.nn.sigmoid((preact - thresh) / gate_width)
        active = (preact * gating).astype(jnp.bfloat16)
        ghost_act = (jnp.exp(preact) * dead_flags).astype(jnp.bfloat16)
        preacts.append(preact)
        sides.append(interleave(active, ghost_act, rows))

    def rebuild(block, m):
        left = sides[m][2 * half * block : 2 * half * (block + 1)]
        out = jnp.dot(left, dec[:, :width], preferred_element_type=jnp.float32)
        return out.astype(jnp.bfloat16)

    other_high = [swap_cores(rebuild(3, m)) for m in range(micros)]
    other_low = [swap_cores(rebuild(2, m)) for m in range(micros)]
    high = [rebuild(1, m) for m in range(micros)]
    low = [rebuild(0, m) for m in range(micros)]
    summed = reduce_stages(low, high, other_low, other_high)
    shares = []
    for m in range(micros):
        residual = own[m].astype(jnp.float32) - summed[m][:rows]
        ghost = summed[m][rows:]
        rr = jnp.sum(residual * residual, axis=1, keepdims=True)
        gg = jnp.sum(ghost * ghost, axis=1, keepdims=True)
        rg = jnp.sum(residual * ghost, axis=1, keepdims=True)
        scale = jnp.sqrt(rr + norm_eps) / (2.0 * jnp.sqrt(gg + norm_eps))
        cross = jnp.where(scale > 0.0, scale * (scale * gg - 2.0 * rg), 0.0)
        columns = in_parts(scale) + in_parts(rr) + in_parts(rr + cross)
        columns = jnp.concatenate(columns, axis=1)
        columns = jnp.pad(columns, ((0, rows), (0, EXTRA - columns.shape[1])))
        both = jnp.concatenate([residual, ghost], axis=0)
        shares.append(jnp.concatenate([both, columns], axis=1).astype(jnp.bfloat16))
    low, other_low, high = gather_stages(jnp.stack(shares))
    sums = jnp.stack([jnp.sum(b[:, width:].astype(jnp.float32), axis=0) for b in low])
    sums, other_low = lax.optimization_barrier((sums, other_low))
    sums = sums + swap_groups(sums, 1)
    sums = sums + swap_groups(sums, 3)
    sums = sums + swap_opposite(sums)
    early = [contract(block, dec, 1) for block in low + other_low]
    high, early, sums = lax.optimization_barrier((high, early, sums))
    sums = sums + swap_cores(sums)
    sums = jnp.stack([jnp.sum(sums[:, 3:6], axis=1), jnp.sum(sums[:, 6:9], axis=1)])
    other_high = [swap_cores(b) for b in high]
    late = [contract(block, dec, 1) for block in high + other_high]
    boths = [b[m] for m in range(micros) for b in (low, high, other_low, other_high)]
    backs = [b[i + m] for m in range(micros) for i in (0, 2) for b in (early, late)]
    pre_grads, dec_pieces = dec_grads(
        rows, sums, thresh.reshape(1, -1), dead_flags.reshape(1, -1), preacts, backs, boths
    )
    enc_pieces = enc_grads(pre_grads, tokens)
    factor = -2.0 / token_total
    dec_parts, enc_parts = reduce_groups(dec_pieces, enc_pieces)
    decoder = update(dec_parts, dec_second, factor, False)
    (enc_parts[2], enc_parts[5]), decoder = lax.optimization_barrier(
        ((enc_parts[2], enc_parts[5]), decoder)
    )
    dec_update, dec_second_new = decoder
    enc_update, enc_second_new = update(enc_parts, enc_second, factor, True)
    losses = sums / token_total
    return (enc_update, enc_second_new, dec_update, dec_second_new, losses)


def solution(mesh):
    renamed = Mesh(mesh.devices, LAT_X)
    in_specs = (
        P(LAT_X, None),
        P(None, LAT_X),
        P(None, "lat"),
        P("lat", None),
        P("lat"),
        P("lat"),
        P("x", "lat"),
        P("lat", "x"),
    )
    out_specs = (P("x", "lat"), P("x", "lat"), P("lat", "x"), P("lat", "x"), P())
    return jax.shard_map(
        shards, mesh=renamed, in_specs=in_specs, out_specs=out_specs, check_vma=False
    )
```

```python
import jax
import jax.numpy as jnp
from jax import lax
from jax.experimental import pallas as pl
from jax.experimental.pallas import tpu as pltpu
from jax.sharding import Mesh
from jax.sharding import PartitionSpec as P

LAT_X = ("lat", "x")


gate_width = 0.1
code_step = 0.1
norm_eps = 1e-06
beta_two = 0.999
adam_eps = 1e-08
adam_count = 2000

QUAD_MASKS = (1, 3, 2)
MASKS = ((1, 3), (3, 1))
STAGES = 2
EXTRA = 128


def adam_second(grads, second):
    renewed = beta_two * second + (1.0 - beta_two) * grads * grads
    correction = 1.0 - beta_two**adam_count
    return (grads / (jnp.sqrt(renewed / correction) + adam_eps), renewed)


def contract(left, right, dim):
    return lax.dot_general(
        left, right, (((dim,), (dim,)), ((), ())), preferred_element_type=jnp.float32
    )


def swap_stage(value, stage, micro):
    mask = MASKS[micro][stage]
    pairs = [(i, i ^ (mask * 8 if i % 2 else mask * 2)) for i in range(32)]
    return lax.ppermute(value, "lat", pairs)


def swap_cores(value):
    return lax.ppermute(value, "lat", [(i, i ^ 1) for i in range(32)])


def exchange_quads(values, crossed=False):
    step = (2, 8) if crossed else (8, 2)
    return [
        lax.ppermute(v, "lat", [(i, i ^ (mask * step[i % 2])) for i in range(32)])
        for v, mask in zip(values, QUAD_MASKS)
    ]


def swap_opposite(value):
    return lax.ppermute(value, "lat", [(i, i ^ (2 * (8 if i % 2 else 2))) for i in range(32)])


def swap_groups(value, mask):
    return lax.ppermute(value, "x", [(i, i ^ mask) for i in range(4)])


def gather_tokens(value, *others):
    spread = [value] + lax.optimization_barrier(exchange_quads([value] * 3))
    block = jnp.concatenate(spread, axis=1)
    near = exchange_quads([block] * 3, crossed=True)
    first = swap_cores(block)
    near, others = lax.optimization_barrier((near, others))
    mine = [block] + near
    theirs = [first] + [swap_cores(v) for v in near]
    tokens = []
    for m in range(2):
        order = [0] + [1 + QUAD_MASKS.index(k) for k in (MASKS[m][0], MASKS[m][1], 2)]
        tokens.append(jnp.concatenate([side[k][m] for side in (mine, theirs) for k in order], axis=0))
    return tokens, others


def gather_stages(value):
    spread = [value] + lax.optimization_barrier(exchange_quads([value] * 3))
    blocks = [jnp.concatenate([v[m] for v in spread], axis=0) for m in range(2)]
    theirs = [swap_stage(b, 0, m) for m, b in enumerate(blocks)]
    low = [jnp.concatenate([b, t], axis=0) for b, t in zip(blocks, theirs)]
    high = [swap_stage(b, 1, m) for m, b in enumerate(low)]
    return low, [swap_cores(b) for b in low], high


def add_rounded(mine, theirs):
    return (mine.astype(jnp.float32) + theirs.astype(jnp.float32)).astype(jnp.bfloat16)


def reduce_stages(low, high, other_low, other_high):
    sent = [add_rounded(a, b) for a, b in zip(high, other_high)]
    theirs = [swap_stage(v, 1, m) for m, v in enumerate(sent)]
    mine = [add_rounded(a, b) for a, b in zip(low, other_low)]
    half = mine[0].shape[0] // 2
    sent = [add_rounded(a[half:], b[half:]) for a, b in zip(mine, theirs)]
    mine = [add_rounded(a[:half], b[:half]) for a, b in zip(mine, theirs)]
    theirs = [swap_stage(v, 0, m) for m, v in enumerate(sent)]
    last = [add_rounded(a, b).reshape(4, -1, a.shape[1]) for a, b in zip(mine, theirs)]
    sent = [jnp.stack([v[k] for v in last]) for k in range(4)]
    got = lax.optimization_barrier(exchange_quads(sent[1:]))
    return sum((v.astype(jnp.float32) for v in got), sent[0].astype(jnp.float32))


def in_parts(value):
    high = lax.reduce_precision(value, 8, 7)
    middle = lax.reduce_precision(value - high, 8, 7)
    return [high, middle, value - high - middle]


def vmem(count):
    return [pl.BlockSpec(memory_space=pltpu.VMEM)] * count


def write_grads(left, rights, width, send_a, send_b, keep_a, keep_b):
    rows = keep_a.shape[1]
    lanes = width if width % 128 else 128
    step = lanes if 4 * width % (2 * lanes) else 2 * lanes
    for start in range(0, 4 * width, step):
        right = jnp.concatenate([r[:, start : start + step] for r in rights], axis=0)
        grads = jnp.dot(left, right, preferred_element_type=jnp.float32)
        for at in range(0, step, lanes):
            slot, column = divmod(start + at, width)
            columns = slice(column, column + lanes)
            top, bottom = grads[:rows, at : at + lanes], grads[rows:, at : at + lanes]
            if slot < 2:
                keep_a[slot, :, columns] = top
            else:
                send_a[(slot - 2) * rows : (slot - 1) * rows, columns] = top.astype(jnp.bfloat16)
            if slot % 2 == 0:
                keep_b[slot // 2, :, columns] = bottom
            else:
                row = slot // 2 * rows
                send_b[row : row + rows, columns] = bottom.astype(jnp.bfloat16)


def grad_shapes(latents, width):
    return [jax.ShapeDtypeStruct((latents, width), jnp.bfloat16)] * 2 + [
        jax.ShapeDtypeStruct((2, latents // 2, width), jnp.float32)
    ] * 2


def dec_kernel(rows, sums_ref, thresh_ref, dead_ref, *refs):
    preacts, backs, boths = refs[0:2], refs[2:10], refs[10:18]
    pre_grads, outs = refs[18:20], refs[20:]
    latents = thresh_ref.shape[1]
    features = boths[0].shape[1] - EXTRA
    tokens = boths[0].shape[0] // 2
    lefts = []
    for micro in range(2):
        ratio = sums_ref[0, micro] / sums_ref[1, micro]
        for i in range(4):
            at = slice(i * tokens, (i + 1) * tokens)
            both, back = boths[4 * micro + i], backs[4 * micro + i]
            preact = preacts[micro][at, :]
            gating = jax.nn.sigmoid((preact - thresh_ref[...]) / gate_width)
            raised = jnp.exp(preact) * dead_ref[...]
            active = (preact * gating).astype(jnp.bfloat16).astype(jnp.float32)
            ghost_act = raised.astype(jnp.bfloat16).astype(jnp.float32)
            extra = both[:, features:].astype(jnp.float32).reshape(-1, 2, rows, EXTRA)
            extra = extra[:, 0].reshape(-1, EXTRA)
            scale = extra[:, 0:1] + extra[:, 1:2] + extra[:, 2:3]
            back = back[...].reshape(-1, 2, rows, latents)
            from_residual = back[:, 0].reshape(-1, latents)
            from_ghost = back[:, 1].reshape(-1, latents)
            scaled = jnp.where(scale > 0.0, scale * from_ghost, 0.0)
            ghost_back = scale * (scaled - from_residual)
            pre_grad = (
                from_residual * (gating + preact * gating * (1.0 - gating) / gate_width)
                - ratio * ghost_back * raised
            )
            pre_grads[micro][at, :] = pre_grad.astype(jnp.bfloat16)
            weighted = ratio * (scale * ghost_act)
            pair = (active + weighted).reshape(-1, 1, rows, latents)
            other = -(scale * weighted).reshape(-1, 1, rows, latents)
            lefts.append(jnp.concatenate([pair, other], axis=1).reshape(-1, latents))
    left = jnp.concatenate(lefts, axis=0).T.astype(jnp.bfloat16)
    write_grads(left, boths, features // 4, *outs)


def dec_grads(rows, sums, thresh, dead_flags, preacts, backs, boths):
    latents = thresh.shape[1]
    width = (boths[0].shape[1] - EXTRA) // 4
    out_shape = [jax.ShapeDtypeStruct(p.shape, jnp.bfloat16) for p in preacts]
    outs = pl.pallas_call(
        lambda *refs: dec_kernel(rows, *refs),
        out_shape=out_shape + grad_shapes(latents, width),
        in_specs=[pl.BlockSpec(memory_space=pltpu.SMEM)] + vmem(20),
        out_specs=vmem(6),
        compiler_params=pltpu.CompilerParams(vmem_limit_bytes=24 * 1024 * 1024),
        cost_estimate=pl.CostEstimate(
            flops=64 * latents * width * boths[0].shape[0],
            bytes_accessed=16 * boths[0].size + 24 * latents * width,
            transcendentals=0,
        ),
        name="decoder_gradient",
    )(sums, thresh, dead_flags, *preacts, *backs, *boths)
    return outs[:2], outs[2:]


def enc_kernel(*refs):
    left = jnp.concatenate([r[...].astype(jnp.float32).T for r in refs[0:2]], axis=1)
    write_grads(left.astype(jnp.bfloat16), refs[2:4], refs[2].shape[1] // 4, *refs[4:])


def enc_grads(pre_grads, tokens):
    latents = pre_grads[0].shape[1]
    width = tokens[0].shape[1] // 4
    return pl.pallas_call(
        enc_kernel,
        out_shape=grad_shapes(latents, width),
        in_specs=vmem(4),
        out_specs=vmem(4),
        compiler_params=pltpu.CompilerParams(vmem_limit_bytes=16 * 1024 * 1024),
        cost_estimate=pl.CostEstimate(
            flops=16 * latents * width * tokens[0].shape[0],
            bytes_accessed=4 * tokens[0].size + 24 * latents * width,
            transcendentals=0,
        ),
        name="encoder_gradient",
    )(*pre_grads, *tokens)


def own_quarter_first(value, dim, group):
    width = value.shape[dim] // 4
    return jnp.concatenate(
        [lax.dynamic_slice_in_dim(value, (group ^ m) * width, width, dim) for m in (0, 1, 3, 2)],
        axis=dim,
    )


def reduce_groups(dec_pieces, enc_pieces):
    rows = dec_pieces[2].shape[1]

    def first(send_a, send_b, keep_a, keep_b):
        return [swap_groups(send_a, 3), swap_groups(send_b, 1)]

    def middle(got, pieces):
        return [
            (kept[1] + half[rows:].astype(jnp.float32)).astype(jnp.bfloat16)
            for half, kept in zip(got, pieces[2:])
        ]

    def last(sent):
        return [swap_groups(sent[0], 1), swap_groups(sent[1], 3)]

    def parts(pieces, got, end):
        return [v for i in range(2) for v in (pieces[2 + i], got[i], end[i])]

    dec_got, enc_got = first(*dec_pieces), first(*enc_pieces)
    dec_sent = middle(dec_got, dec_pieces)
    dec_end = last(dec_sent)
    enc_got, _ = lax.optimization_barrier((enc_got, dec_sent))
    enc_end = last(middle(enc_got, enc_pieces))
    return parts(dec_pieces, dec_got, dec_end), parts(enc_pieces, enc_got, enc_end)


def update_kernel(factor, turned, *refs):
    keep_a, got_a, last_a, keep_b, got_b, last_b, second_ref = refs[0:7]
    update_out, renewed_out, update_ref, renewed_ref, sems = refs[7:]
    rows, width = last_a.shape

    def total(keep, got, last, at):
        first = slice(at[0].start, at[0].stop)
        return keep[0, first, at[1]] + (
            got[first, at[1]].astype(jnp.float32) + last[first, at[1]].astype(jnp.float32)
        )

    copies = []
    count = sems.shape[1]
    size = second_ref.shape[0] // count
    for i in range(count):
        block = slice(i * size, (i + 1) * size)
        if turned:
            at = (slice(0, rows), block)
            grads = jnp.concatenate(
                [total(keep_a, got_a, last_a, at), total(keep_b, got_b, last_b, at)], axis=0
            ).T
        else:
            start = i * size % rows
            at = (slice(start, start + size), slice(0, width))
            half = (keep_a, got_a, last_a) if i * size < rows else (keep_b, got_b, last_b)
            grads = total(*half, at)
        values = adam_second(grads * factor, second_ref[block, :])
        for k, (value, ref, out) in enumerate(
            zip(values, (update_ref, renewed_ref), (update_out, renewed_out))
        ):
            ref[block, :] = value
            copy = pltpu.make_async_copy(ref.at[block, :], out.at[block, :], sems.at[k, i])
            copy.start()
            copies.append(copy)
    for copy in copies:
        copy.wait()


def update(parts, second, factor, turned):
    count = (7 if second.shape[0] % 896 == 0 else 1) if turned else 4
    return pl.pallas_call(
        lambda *refs: update_kernel(factor, turned, *refs),
        out_shape=[jax.ShapeDtypeStruct(second.shape, jnp.float32)] * 2,
        in_specs=vmem(7),
        out_specs=[pl.BlockSpec(memory_space=pl.ANY)] * 2,
        scratch_shapes=[
            pltpu.VMEM(second.shape, jnp.float32),
            pltpu.VMEM(second.shape, jnp.float32),
            pltpu.SemaphoreType.DMA((2, count)),
        ],
        compiler_params=pltpu.CompilerParams(vmem_limit_bytes=12 * 1024 * 1024),
        cost_estimate=pl.CostEstimate(
            flops=20 * second.size, bytes_accessed=20 * second.size, transcendentals=second.size
        ),
        name="encoder_update" if turned else "decoder_update",
    )(*parts, second)


def interleave(first, second, rows):
    width = first.shape[1]
    both = jnp.stack([first.reshape(-1, rows, width), second.reshape(-1, rows, width)], axis=1)
    return both.reshape(-1, width)


def shards(
    buffer, row_ids, enc_weight, dec_weight, threshold_codes, dead_mask, enc_second, dec_second
):
    micros, rows = row_ids.shape
    token_total = micros * rows * 128
    group = lax.axis_index("x")
    thresh = code_step * threshold_codes.astype(jnp.float32)
    dead_flags = dead_mask.astype(jnp.float32)
    enc = own_quarter_first(enc_weight, 0, group)
    dec = own_quarter_first(dec_weight, 1, group)
    dec = jnp.pad(dec, ((0, 0), (0, EXTRA)))
    own = jnp.stack([own_quarter_first(buffer[row_ids[m]], 1, group) for m in range(micros)])
    tokens, (enc, dec) = gather_tokens(own, enc, dec)
    width = enc.shape[0]
    half = tokens[0].shape[0] // 4
    preacts = []
    sides = []
    for m in range(micros):
        preact = jnp.dot(tokens[m], enc, preferred_element_type=jnp.float32)
        gating = jax.nn.sigmoid((preact - thresh) / gate_width)
        active = (preact * gating).astype(jnp.bfloat16)
        ghost_act = (jnp.exp(preact) * dead_flags).astype(jnp.bfloat16)
        preacts.append(preact)
        sides.append(interleave(active, ghost_act, rows))

    def rebuild(block, m):
        left = sides[m][2 * half * block : 2 * half * (block + 1)]
        out = jnp.dot(left, dec[:, :width], preferred_element_type=jnp.float32)
        return out.astype(jnp.bfloat16)

    other_high = [swap_cores(rebuild(3, m)) for m in range(micros)]
    other_low = [swap_cores(rebuild(2, m)) for m in range(micros)]
    high = [rebuild(1, m) for m in range(micros)]
    low = [rebuild(0, m) for m in range(micros)]
    summed = reduce_stages(low, high, other_low, other_high)
    shares = []
    for m in range(micros):
        residual = own[m].astype(jnp.float32) - summed[m][:rows]
        ghost = summed[m][rows:]
        rr = jnp.sum(residual * residual, axis=1, keepdims=True)
        gg = jnp.sum(ghost * ghost, axis=1, keepdims=True)
        rg = jnp.sum(residual * ghost, axis=1, keepdims=True)
        scale = jnp.sqrt(rr + norm_eps) / (2.0 * jnp.sqrt(gg + norm_eps))
        cross = jnp.where(scale > 0.0, scale * (scale * gg - 2.0 * rg), 0.0)
        columns = in_parts(scale) + in_parts(rr) + in_parts(rr + cross)
        columns = jnp.concatenate(columns, axis=1)
        columns = jnp.pad(columns, ((0, rows), (0, EXTRA - columns.shape[1])))
        both = jnp.concatenate([residual, ghost], axis=0)
        shares.append(jnp.concatenate([both, columns], axis=1).astype(jnp.bfloat16))
    low, other_low, high = gather_stages(jnp.stack(shares))
    sums = jnp.stack([jnp.sum(b[:, width:].astype(jnp.float32), axis=0) for b in low])
    sums, other_low = lax.optimization_barrier((sums, other_low))
    sums = sums + swap_groups(sums, 1)
    sums = sums + swap_groups(sums, 3)
    sums = sums + swap_opposite(sums)
    early = [contract(block, dec, 1) for block in low + other_low]
    high, early, sums = lax.optimization_barrier((high, early, sums))
    sums = sums + swap_cores(sums)
    sums = jnp.stack([jnp.sum(sums[:, 3:6], axis=1), jnp.sum(sums[:, 6:9], axis=1)])
    other_high = [swap_cores(b) for b in high]
    late = [contract(block, dec, 1) for block in high + other_high]
    boths = [b[m] for m in range(micros) for b in (low, high, other_low, other_high)]
    backs = [b[i + m] for m in range(micros) for i in (0, 2) for b in (early, late)]
    pre_grads, dec_pieces = dec_grads(
        rows, sums, thresh.reshape(1, -1), dead_flags.reshape(1, -1), preacts, backs, boths
    )
    enc_pieces = enc_grads(pre_grads, tokens)
    factor = -2.0 / token_total
    dec_parts, enc_parts = reduce_groups(dec_pieces, enc_pieces)
    decoder = update(dec_parts, dec_second, factor, False)
    (enc_parts[2], enc_parts[5]), decoder = lax.optimization_barrier(
        ((enc_parts[2], enc_parts[5]), decoder)
    )
    dec_update, dec_second_new = decoder
    enc_update, enc_second_new = update(enc_parts, enc_second, factor, True)
    losses = sums / token_total
    return (enc_update, enc_second_new, dec_update, dec_second_new, losses)


def solution(mesh):
    renamed = Mesh(mesh.devices, LAT_X)
    in_specs = (
        P(LAT_X, None),
        P(None, LAT_X),
        P(None, "lat"),
        P("lat", None),
        P("lat"),
        P("lat"),
        P("x", "lat"),
        P("lat", "x"),
    )
    out_specs = (P("x", "lat"), P("x", "lat"), P("lat", "x"), P("lat", "x"), P())
    return jax.shard_map(
        shards, mesh=renamed, in_specs=in_specs, out_specs=out_specs, check_vma=False
    )
```
